32 devices in a mesh: sym: 2 (over core), rad: 16 (over z, y, x).
Axes of the slice: x: 2, y: 2, z: 4, core: 2. Of those that a mesh axis runs over, the one named last changes fastest.
Arguments:
- start_amplitudes: float32 [2, 768, 16, 128], P('sym', None, 'rad'), may hold values from -6 to 6
- coupling: bfloat16 [2, 3, 768, 3, 768], P('sym'), may hold values from -0.078125 to 0.078125
- block_pattern: int32 [2, 6, 3, 6], P('sym'), may hold values 0 or 1
- counts: int32 [2], P('sym'), may hold values from 256 to 768, as said below
- radial_terms: float32 [3, 256], P(None, 'rad'), may hold values from 0.5 to 2
- energy: float32 [2, 768], P('sym'), may hold values from -3 to 3
- potential: float32 [256], replicated, may hold values from -3.140625 to 3.140625
- element_matrices: float32 [2, 2, 128, 128], replicated, may hold values from -0.375 to 0.375
Outputs:
- end_amplitudes: float32 [2, 768, 16, 128], P('sym', None, 'rad')
The draws below stay inside these ranges and needn't reach their ends.
Inputs may be any that keep to these rules, and one draw needn't show every extreme that they name: `counts`: some symmetry has exactly 768 live channels in every draw.
All inputs are finite; a program needn't handle non-finite values. No bound on the sum of `block_pattern` on one device may be relied on, other than what follows from the above.
Results may differ from the reference program's by a relative error of at most 0.0029.
Values may be sent and summed in bfloat16 or wider, within the bound.
No kernel may reach another device: no remote copies, remote signals or barrier semaphores. Data moves between devices by JAX's collectives and lax.ppermute only.
A program may use at most 128 MiB of HBM per device.

```python
import math
import jax
import jax.numpy as jnp
from jax import lax

CHANNELS = 768
ORDERS = 3
PATTERN_TILE = 128
ELEM_WIDTH = 128
RAD_DEV = 16
STATES = 4
TIME_STEPS = 2
SYMMETRIES = 2
RAD_BLOCKS = 16
COLUMNS = 128
POINTS = 256
ELEMENTS = 2


def draw_counts(key, part):
    first_key = jax.random.fold_in(key, 11)
    second_key = jax.random.fold_in(key, 23)
    values = jax.random.randint(first_key, (SYMMETRIES,), CHANNELS // 3, CHANNELS + 1)
    chosen = jax.random.randint(second_key, (), 0, SYMMETRIES)
    return jnp.where(jnp.arange(SYMMETRIES) == chosen, CHANNELS, values).astype(jnp.int32)


def set_ends(values, key, least, largest):
    shape = values.shape
    index_at = [jax.random.randint(jax.random.fold_in(key, axis), (), 0, shape[axis]) for axis in range(len(shape))]
    values = values.at[tuple(index_at)].set(least)
    longest = shape.index(max(shape))
    index_at[longest] = (index_at[longest] + 1) % shape[longest]
    return values.at[tuple(index_at)].set(largest)


def block_levels(key, dims, shards, least, top_value):
    level = 1.0
    for dim, shards_of in shards:
        draws = jax.random.uniform(jax.random.fold_in(jax.random.fold_in(key, 6), dim), (shards_of,), jnp.float32, least / len(shards), top_value / len(shards))
        level = level * jnp.repeat(jnp.exp(draws), dims[dim] // shards_of).reshape((-1,) + (1,) * (len(dims) - 1 - dim))
    return level


def centred(stream_key, dims, scale, most, pieces=(), kind=jnp.bfloat16):
    values = jax.random.normal(stream_key, dims, jnp.float32) * scale
    if len(pieces) > 0:
        values = block_levels(stream_key, dims, pieces, -0.22, 0.18) * values
    return jnp.clip(values, min=-most, max=most).astype(kind)


def setup_inputs(seed: int = 0) -> dict:
    key_of = jax.random.split(jax.random.key(seed), 9)
    start_amplitudes = centred(key_of[0], (SYMMETRIES, CHANNELS, RAD_BLOCKS, COLUMNS), 1.0, 6.0, ((0, 2), (2, 16)), jnp.float32)
    coupling = centred(key_of[1], (SYMMETRIES, ORDERS, CHANNELS, 3, CHANNELS), (3 * ORDERS * CHANNELS) ** -0.5, 0.078125, ((0, 2),))
    block_pattern = set_ends((jax.random.randint(key_of[2], (SYMMETRIES, CHANNELS // PATTERN_TILE, 3, CHANNELS // PATTERN_TILE), 0, 4) < 3).astype(jnp.int32), jax.random.fold_in(key_of[2], 1), 0, 1)
    counts = draw_counts(jax.random.fold_in(key_of[8], 71), 0)
    radial_terms = jnp.clip(jnp.exp(math.log(2.0) - 1.3862944 * jax.random.uniform(key_of[4], (ORDERS, POINTS), jnp.float32) ** block_levels(key_of[4], (ORDERS, POINTS), ((1, 16),), -0.2, 0.2)), 0.5, 2.0)
    energy = jnp.clip(jax.random.uniform(key_of[5], (SYMMETRIES, CHANNELS), jnp.float32, -3.0, 3.0) * block_levels(key_of[5], (SYMMETRIES, CHANNELS), ((0, 2),), -0.4, 0.0), -3.0, 3.0)
    potential = jnp.clip(jax.random.uniform(key_of[6], (POINTS,), jnp.float32, -3.140625, 3.140625), -3.140625, 3.140625)
    element_matrices = centred(key_of[7], (2, ELEMENTS, ELEM_WIDTH, ELEM_WIDTH), (2 * ELEM_WIDTH) ** -0.5, 0.375, (), jnp.float32)
    return {"start_amplitudes": start_amplitudes, "coupling": coupling, "block_pattern": block_pattern, "counts": counts, "radial_terms": radial_terms, "energy": energy, "potential": potential, "element_matrices": element_matrices}


step_length = 0.8


def element_product(real_part, imag_part, matrices):
    shape_in = real_part.shape
    elements = matrices.shape[1]
    width = matrices.shape[2]
    real_blocks = real_part.reshape(shape_in[:-1] + (elements, width))
    imag_blocks = imag_part.reshape(shape_in[:-1] + (elements, width))
    highest = lax.Precision.HIGHEST
    out_real = jnp.einsum("abnej,eij->abnei", real_blocks, matrices[0], precision=highest) - jnp.einsum("abnej,eij->abnei", imag_blocks, matrices[1], precision=highest)
    out_imag = jnp.einsum("abnej,eij->abnei", imag_blocks, matrices[0], precision=highest) + jnp.einsum("abnej,eij->abnei", real_blocks, matrices[1], precision=highest)
    return out_real.reshape(shape_in), out_imag.reshape(shape_in)


def radial_half(channel_block, cosine, sine, matrices):
    real_part = channel_block[:, :, :, 0, :]
    imag_part = channel_block[:, :, :, 1, :]
    turned_real = real_part * cosine + imag_part * sine
    turned_imag = imag_part * cosine - real_part * sine
    out_real, out_imag = element_product(turned_real, turned_imag, matrices)
    return jnp.stack((out_real, out_imag), axis=3)


def to_points(stored):
    split = stored.reshape(SYMMETRIES, CHANNELS, RAD_BLOCKS, STATES, 2, RAD_DEV)
    return split.transpose(0, 1, 3, 4, 2, 5).reshape(SYMMETRIES, CHANNELS, STATES, 2, POINTS)


def to_blocks(amplitudes):
    split = amplitudes.reshape(SYMMETRIES, CHANNELS, STATES, 2, RAD_BLOCKS, RAD_DEV)
    return split.transpose(0, 1, 4, 2, 3, 5).reshape(SYMMETRIES, CHANNELS, RAD_BLOCKS, COLUMNS)


def reference(start_amplitudes, coupling, block_pattern, counts, radial_terms, energy, potential, element_matrices):
    live_rows = (jnp.arange(CHANNELS, dtype=jnp.int32)[None, :] < counts[:, None]).astype(jnp.float32)[:, :, None, None, None]
    pattern = jnp.repeat(jnp.repeat(block_pattern, PATTERN_TILE, axis=1), PATTERN_TILE, axis=3).astype(jnp.bfloat16)
    weights = coupling * pattern[:, None]
    angles = energy[:, :, None] + potential[None, None, :]
    cosine = jnp.cos(angles)[:, :, None, :]
    sine = jnp.sin(angles)[:, :, None, :]

    def coupled_term(current):
        padded = jnp.pad(current.astype(jnp.bfloat16), ((1, 1), (0, 0), (0, 0), (0, 0), (0, 0)))

        def one_symmetry(index):
            widened = lax.dynamic_slice_in_dim(padded, index, 3, 0).reshape(3 * CHANNELS, STATES * 2 * POINTS)
            matrix = lax.dynamic_index_in_dim(weights, index, 0, keepdims=False).reshape(ORDERS * CHANNELS, 3 * CHANNELS)
            product = jnp.dot(matrix, widened, preferred_element_type=jnp.float32)
            product = product.reshape(ORDERS, CHANNELS, STATES, 2, POINTS)
            return jnp.sum(product * radial_terms[:, None, None, None, :], axis=0)

        return lax.map(one_symmetry, jnp.arange(SYMMETRIES, dtype=jnp.int32)) * live_rows

    def taylor(amplitudes):
        summed = amplitudes
        current = amplitudes
        for order_index in range(1, 4):
            coupled = coupled_term(current)
            factor = step_length / order_index
            current = jnp.stack((factor * coupled[:, :, :, 1], -factor * coupled[:, :, :, 0]), axis=3)
            summed = summed + current
        return summed

    amplitudes = to_points(start_amplitudes) * live_rows
    for step_index in range(TIME_STEPS):
        amplitudes = radial_half(amplitudes, cosine, sine, element_matrices)
        amplitudes = taylor(amplitudes)
        amplitudes = radial_half(amplitudes, cosine, sine, element_matrices)
    return to_blocks(amplitudes)
```

```python
import jax
import jax.numpy as jnp
from jax import lax
from jax.experimental import pallas as pl
from jax.experimental.pallas import tpu as pltpu
from jax.sharding import PartitionSpec as P

TIME_STEPS = 2


step_length = 0.8


def extended(x, sides, width):
    for axis, dim in sides:
        size, length = (lax.axis_size(axis), x.shape[dim])
        up = [(i, (i + 1) % size) for i in range(size - 1)]
        down = [(j, i) for i, j in up]
        last = lax.slice_in_dim(x, length - width, length, axis=dim)
        initial = lax.slice_in_dim(x, 0, width, axis=dim)
        before = lax.ppermute(last, axis, up)
        after = lax.ppermute(initial, axis, down)
        x = jnp.concatenate([before, x, after], axis=dim)
    return x


def element_product(real_part, imag_part, matrices):
    shape_in = real_part.shape
    elements = matrices.shape[1]
    width = matrices.shape[2]
    real_blocks = real_part.reshape(shape_in[:-1] + (elements, width))
    imag_blocks = imag_part.reshape(shape_in[:-1] + (elements, width))
    highest = lax.Precision.HIGHEST
    out_real = jnp.einsum(
        "abnej,eij->abnei", real_blocks, matrices[0], precision=highest
    ) - jnp.einsum("abnej,eij->abnei", imag_blocks, matrices[1], precision=highest)
    out_imag = jnp.einsum(
        "abnej,eij->abnei", imag_blocks, matrices[0], precision=highest
    ) + jnp.einsum("abnej,eij->abnei", real_blocks, matrices[1], precision=highest)
    return (out_real.reshape(shape_in), out_imag.reshape(shape_in))


def radial_half(channel_block, cosine, sine, matrices):
    real_part = channel_block[:, :, :, 0, :]
    imag_part = channel_block[:, :, :, 1, :]
    turned_real = real_part * cosine + imag_part * sine
    turned_imag = imag_part * cosine - real_part * sine
    out_real, out_imag = element_product(turned_real, turned_imag, matrices)
    return jnp.stack((out_real, out_imag), axis=3)


def halo_shards(
    start_amplitudes,
    coupling,
    block_pattern,
    counts,
    radial_terms,
    energy,
    potential,
    element_matrices,
):
    capacity = coupling.shape[2]
    orders = coupling.shape[1]
    tile_size = capacity // block_pattern.shape[1]
    pattern = jnp.repeat(jnp.repeat(block_pattern[0], tile_size, axis=0), tile_size, axis=2).astype(
        jnp.bfloat16
    )
    weights = (coupling[0] * pattern[None]).reshape(orders * capacity, 3 * capacity)
    live_rows = (
        (jnp.arange(capacity, dtype=jnp.int32) < counts[0])
        .astype(jnp.float32)
        .reshape(1, capacity, 1, 1)
    )
    columns = start_amplitudes.shape[3]
    block_points = radial_terms.shape[1]
    states = columns // (2 * block_points)
    points = potential.shape[0]
    blocks_all = points // block_points
    per_device = capacity // lax.axis_size("rad")
    first_row = lax.axis_index("rad") * per_device
    local_energy = lax.dynamic_slice_in_dim(energy[0], first_row, per_device)
    angles = local_energy[:, None] + potential[None, :]
    cosine = jnp.cos(angles)[None, :, None, :]
    sine = jnp.sin(angles)[None, :, None, :]
    radial_rows = jnp.broadcast_to(
        radial_terms[:, None, None, :], (orders, states, 2, block_points)
    ).reshape(orders, 1, columns)
    out_index = jnp.arange(columns, dtype=jnp.int32)
    out_part = out_index // block_points % 2
    in_index = out_index[:, None]
    swap_sign = jnp.where(
        (in_index == out_index[None, :] + block_points) & (out_part[None, :] == 0), 1.0, 0.0
    )
    swap_sign = swap_sign - jnp.where(
        (in_index == out_index[None, :] - block_points) & (out_part[None, :] == 1), 1.0, 0.0
    )
    swap_sign = swap_sign.astype(jnp.float32)

    def coupled_term(current):
        sent = current.astype(jnp.bfloat16)
        widened = extended(sent, (("sym", 0),), 1)
        product = jnp.dot(
            weights, widened.reshape(3 * capacity, columns), preferred_element_type=jnp.float32
        )
        product = product.reshape(orders, capacity, columns)
        coupled = jnp.sum(product * radial_rows, axis=0)
        return coupled.reshape(1, capacity, 1, columns) * live_rows

    def relay_block(amplitudes, repeats):
        channel_block = lax.all_to_all(amplitudes, "rad", split_axis=1, concat_axis=2, tiled=True)
        items = channel_block.shape[0]
        spread = channel_block.reshape(items, per_device, blocks_all, states, 2, block_points)
        spread = spread.transpose(0, 1, 3, 4, 2, 5).reshape(items, per_device, states, 2, points)
        for repeat_index in range(repeats):
            spread = radial_half(spread, cosine, sine, element_matrices)
        folded = spread.reshape(items, per_device, states, 2, blocks_all, block_points)
        moved = folded.transpose(0, 1, 4, 2, 3, 5).reshape(items, per_device, blocks_all, columns)
        return lax.all_to_all(moved, "rad", split_axis=2, concat_axis=1, tiled=True)

    amplitudes = start_amplitudes * live_rows
    amplitudes = relay_block(amplitudes, 1)
    for step_index in range(TIME_STEPS):
        first = step_length * coupled_term(amplitudes)
        second = step_length / 2.0 * coupled_term(first)
        third = step_length / 3.0 * coupled_term(second)
        even_sum = amplitudes - second
        odd_sum = (first - third).reshape(capacity, columns)
        turned = jnp.dot(
            odd_sum, swap_sign, precision=lax.Precision.HIGHEST, preferred_element_type=jnp.float32
        )
        amplitudes = even_sum + turned.reshape(1, capacity, 1, columns)
        amplitudes = relay_block(amplitudes, 1 if step_index + 1 == TIME_STEPS else 2)
    return amplitudes


f32 = jnp.float32
bf16 = jnp.bfloat16
f16 = jnp.float16
NT = (((1,), (1,)), ((), ()))


def halves(x):
    high = x.astype(bf16)
    return high, (x - high.astype(f32)).astype(bf16)


def split_dot(a, b):
    a0, a1 = halves(a)
    b0, b1 = halves(b)

    def mm(x, y):
        return lax.dot_general(x, y, NT, preferred_element_type=f32)

    return mm(a0, b0) + (mm(a0, b1) + mm(a1, b0))


def pack_kernel(count_ref, start_ref, radial_ref, out_ref):
    capacity, columns = start_ref.shape
    states, rows, width = out_ref.shape
    row = lax.broadcasted_iota(jnp.int32, (capacity, columns), 0)
    live = jnp.where(row < count_ref[0], start_ref[...], 0.0)
    out_ref[:, :, :capacity] = live.T.reshape(states, rows, capacity)
    for state in range(states):
        out_ref[state, :, capacity:] = radial_ref[...]


def unpack_kernel(in_ref, out_ref):
    states, rows, capacity = in_ref.shape
    out_ref[...] = in_ref[...].reshape(states * rows, capacity).astype(f32).T


def steps_kernel(
    orders,
    block,
    info_ref,
    own_w,
    other_w,
    own_x,
    other_x,
    phase_ref,
    turn_ref,
    matrix_ref,
    out_ref,
    weights,
    current,
    total,
    factors,
    phases,
    one_half,
    two_half,
    sems,
):
    tiles = weights.shape[1]
    tile = weights.shape[3]
    capacity = tiles * tile
    columns = current.shape[2]
    width = columns // 2
    me = info_ref[0]
    part = info_ref[1]
    per_slot = tiles * 3 * tiles

    def fetch(a, i, b):
        k = 1 if a == b else (2 - 2 * me if a == 0 else 2 * me)
        source = own_w if a == 0 else other_w
        return pltpu.make_async_copy(
            source.at[:, k, i * tile : (i + 1) * tile, :],
            weights.at[a, i, :, :, b * capacity : (b + 1) * capacity],
            sems.at[a, i, b],
        )

    for a in range(2):
        for i in range(tiles):
            for b in range(2):
                fetch(a, i, b).start()

    m0 = matrix_ref[0]
    m1 = matrix_ref[1]
    cosine = turn_ref[0:1]
    sine = turn_ref[1:2]
    k0 = m0 * cosine + m1 * sine
    k1 = m1 * cosine - m0 * sine

    def store_pair(ref, real, imag):
        ref[:width, :width] = real
        ref[:width, width:] = -imag
        ref[width:, :width] = imag
        ref[width:, width:] = real

    store_pair(one_half, k0, k1)
    highest = lax.Precision.HIGHEST
    square = lambda x, y: jnp.dot(x, y, precision=highest, preferred_element_type=f32)
    store_pair(two_half, square(k0, k0) - square(k1, k1), square(k0, k1) + square(k1, k0))

    phases[...] = phase_ref[...].T

    def rotated(v, a, col):
        c = phases[:, 4 * a + col : 4 * a + col + 1]
        s = phases[:, 4 * a + col + 1 : 4 * a + col + 2]
        real, imag = v[:, :width], v[:, width:]
        return jnp.concatenate([real * c + imag * s, imag * c - real * s], axis=1)

    def begin(a, v):
        total[a * capacity : (a + 1) * capacity] = v
        current[0, a * capacity : (a + 1) * capacity] = v.astype(bf16)

    for a, x_ref in enumerate((own_x, other_x)):
        x = x_ref[...]
        blocks = x.shape[0] // (2 * block)
        pieces = [
            x[(2 * n + p) * block : (2 * n + p + 1) * block] for p in range(2) for n in range(blocks)
        ]
        turned = jnp.concatenate(pieces, axis=0).T
        begin(a, rotated(split_dot(turned[:capacity], one_half[...]), a, 0))
        if a == 0:
            for l in range(orders):
                rows = turned[capacity + 3 * l : capacity + 3 * l + 3]
                factors[l : l + 1] = rows[0:1] + (rows[1:2] + rows[2:3] / 2048.0) / 2048.0

    def couple(slot, factor, ready):
        radial = [factors[l : l + 1] * factor for l in range(orders)]
        for a in range(2):
            count = info_ref[2 + a]
            for i in range(tiles):
                if not ready:
                    for b in range(2):
                        fetch(a, i, b).wait()
                    for b in range(2):
                        k = 1 if a == b else (2 - 2 * me if a == 0 else 2 * me)
                        for j in range(tiles):
                            present = info_ref[4 + a * per_slot + (i * 3 + k) * tiles + j]
                            first = b * capacity + j * tile

                            @pl.when(present == 0)
                            def _():
                                weights[a, i, :, :, first : first + tile] = jnp.zeros(
                                    (orders, tile, tile), bf16
                                )

                w = weights[a, i].reshape(orders * tile, 2 * capacity)
                product = jnp.dot(w, current[slot], preferred_element_type=f32)
                u = product[:tile] * radial[0]
                for l in range(1, orders):
                    u = u + product[l * tile : (l + 1) * tile] * radial[l]
                row = lax.broadcasted_iota(jnp.int32, u.shape, 0) + i * tile
                u = jnp.where(row < count, u, 0.0)
                term = jnp.concatenate([u[:, width:], -u[:, :width]], axis=1)
                first = a * capacity + i * tile
                total[first : first + tile] += term
                current[1 - slot, first : first + tile] = term.astype(bf16)

    step_length_over = lambda k: jnp.where(
        k == 0, step_length, jnp.where(k == 1, step_length / 2.0, step_length / 3.0)
    )
    couple(0, step_length, False)

    def later(index, carry):
        k = lax.rem(index, 3)
        slot = lax.rem(index, 2)

        @pl.when(k == 0)
        def _():
            for a in range(2):
                v = total[a * capacity : (a + 1) * capacity]
                v = rotated(split_dot(v, two_half[...]), a, 2)
                total[a * capacity : (a + 1) * capacity] = v
                current[slot, a * capacity : (a + 1) * capacity] = v.astype(bf16)

        couple(slot, step_length_over(k), True)
        return carry

    lax.fori_loop(1, 3 * TIME_STEPS, later, 0)

    final = rotated(total[:capacity], 0, 0)
    pieces = out_ref.shape[0]
    spread = width // (block * pieces)
    for m in range(pieces):
        for p in range(2):
            first = pl.multiple_of(p * width + (m * spread + part) * block, block)
            two_half[(2 * m + p) * block : (2 * m + p + 1) * block] = one_half[pl.ds(first, block)]
    result = split_dot(two_half[: 2 * pieces * block], final)
    out_ref[...] = result.astype(bf16).reshape(out_ref.shape)


def pair_shards(
    start_amplitudes,
    coupling,
    block_pattern,
    counts,
    radial_terms,
    energy,
    potential,
    element_matrices,
):
    orders, capacity = coupling.shape[1:3]
    tiles = block_pattern.shape[1]
    tile = capacity // tiles
    columns = start_amplitudes.shape[3]
    block = radial_terms.shape[1]
    width = element_matrices.shape[2]
    elements = element_matrices.shape[1]
    states = columns // (2 * block)
    group = width // block
    spread = group // states
    rows = 2 * block
    vmem = pl.BlockSpec(memory_space=pltpu.VMEM)
    smem = pl.BlockSpec(memory_space=pltpu.SMEM)
    anywhere = pl.BlockSpec(memory_space=pl.ANY)
    swap = [(0, 1), (1, 0)]
    place = lax.axis_index("rad")
    me = lax.axis_index("sym")
    element = place // group

    other_coupling = lax.ppermute(coupling, "sym", swap)
    angle = energy[0]
    phase = jnp.stack([jnp.cos(angle), jnp.sin(angle), jnp.cos(2.0 * angle), jnp.sin(2.0 * angle)])
    integers = jnp.concatenate([counts, block_pattern.reshape(-1)]).astype(f32)
    padded = -(-integers.shape[0] // capacity) * capacity
    small = jnp.concatenate(
        [phase, jnp.pad(integers, (0, padded - integers.shape[0])).reshape(-1, capacity)]
    )
    other_small = lax.ppermute(small, "sym", swap)
    other_integers = other_small[4:].reshape(-1)[: integers.shape[0]].astype(jnp.int32)
    info = jnp.concatenate(
        [
            jnp.stack([me, place % spread, counts[0], other_integers[0]]).astype(jnp.int32),
            block_pattern.reshape(-1),
            other_integers[1:],
        ]
    )
    lanes = 128
    phases = jnp.concatenate(
        [phase, other_small[:4], jnp.zeros((lanes - 8, capacity), f32)]
    )
    radii = lax.dynamic_slice_in_dim(potential, element * width, width)
    turn = jnp.stack([jnp.cos(radii), jnp.sin(radii)])
    matrices = lax.dynamic_index_in_dim(element_matrices, element, 1, keepdims=False)

    high = lax.reduce_precision(radial_terms, 8, 10)
    rest = (radial_terms - high) * 2048.0
    middle = lax.reduce_precision(rest, 8, 10)
    low = (rest - middle) * 2048.0
    pieces = jnp.stack([high, middle, low], axis=1).reshape(3 * orders, block).T
    radial = jnp.pad(jnp.tile(pieces, (2, 1)), ((0, 0), (0, lanes - 3 * orders)))

    packed = pl.pallas_call(
        pack_kernel,
        out_shape=jax.ShapeDtypeStruct((states, rows, capacity + lanes), f32),
        in_specs=[smem, vmem, vmem],
        out_specs=vmem,
        name="pack",
    )(counts, start_amplitudes.reshape(capacity, columns), radial)
    wide = [[e * group + d for d in range(group)] for e in range(elements)]
    gathered = lax.all_to_all(
        jnp.repeat(packed.astype(f16), spread, axis=0), "rad", split_axis=0, concat_axis=0, tiled=True, axis_index_groups=wide
    ).reshape(group * rows, capacity + lanes)
    other_gathered = lax.ppermute(gathered, "sym", swap)

    def by_order(x):
        return x[0].transpose(0, 2, 1, 3)

    scratch = [
        pltpu.VMEM((2, tiles, orders, tile, 2 * capacity), bf16),
        pltpu.VMEM((2, 2 * capacity, 2 * width), bf16),
        pltpu.VMEM((2 * capacity, 2 * width), f32),
        pltpu.VMEM((8, 2 * width), f32),
        pltpu.VMEM((capacity, lanes), f32),
        pltpu.VMEM((2 * width, 2 * width), f32),
        pltpu.VMEM((2 * width, 2 * width), f32),
        pltpu.SemaphoreType.DMA((2, tiles, 2)),
    ]

    def body(*refs):
        steps_kernel(orders, block, *refs)

    result = pl.pallas_call(
        body,
        out_shape=jax.ShapeDtypeStruct((states, rows, capacity), bf16),
        in_specs=[smem, anywhere, anywhere, vmem, vmem, vmem, vmem, vmem],
        out_specs=vmem,
        scratch_shapes=scratch,
        compiler_params=pltpu.CompilerParams(vmem_limit_bytes=48 << 20),
        name="steps",
    )(
        info,
        by_order(coupling),
        by_order(other_coupling),
        gathered.astype(f32),
        other_gathered.astype(f32),
        phases,
        turn,
        matrices,
    )
    narrow = [
        [e * group + n * spread + d for n in range(states)]
        for e in range(elements)
        for d in range(spread)
    ]
    returned = lax.all_to_all(
        result, "rad", split_axis=0, concat_axis=0, tiled=True, axis_index_groups=narrow
    )
    out = pl.pallas_call(
        unpack_kernel,
        out_shape=jax.ShapeDtypeStruct((capacity, columns), f32),
        in_specs=[vmem],
        out_specs=vmem,
        name="unpack",
    )(returned)
    return out.reshape(start_amplitudes.shape)


def solution(mesh):
    def program(*args):
        states = args[0].shape[3] // (2 * args[4].shape[1])
        group = args[7].shape[2] // args[4].shape[1]
        paired = mesh.shape["sym"] == 2 and group % states == 0
        return pair_shards(*args) if paired else halo_shards(*args)

    return jax.shard_map(
        program,
        mesh=mesh,
        in_specs=(
            P("sym", None, "rad", None),
            P("sym", None, None, None, None),
            P("sym", None, None, None),
            P("sym"),
            P(None, "rad"),
            P("sym", None),
            P(),
            P(),
        ),
        out_specs=P("sym", None, "rad", None),
        check_vma=False,
    )
```

```python
import jax
import jax.numpy as jnp
from jax import lax
from jax.experimental import pallas as pl
from jax.experimental.pallas import tpu as pltpu
from jax.sharding import PartitionSpec as P

TIME_STEPS = 2


step_length = 0.8


def extended(x, sides, width):
    for axis, dim in sides:
        size, length = (lax.axis_size(axis), x.shape[dim])
        up = [(i, (i + 1) % size) for i in range(size - 1)]
        down = [(j, i) for i, j in up]
        last = lax.slice_in_dim(x, length - width, length, axis=dim)
        initial = lax.slice_in_dim(x, 0, width, axis=dim)
        before = lax.ppermute(last, axis, up)
        after = lax.ppermute(initial, axis, down)
        x = jnp.concatenate([before, x, after], axis=dim)
    return x


def element_product(real_part, imag_part, matrices):
    shape_in = real_part.shape
    elements = matrices.shape[1]
    width = matrices.shape[2]
    real_blocks = real_part.reshape(shape_in[:-1] + (elements, width))
    imag_blocks = imag_part.reshape(shape_in[:-1] + (elements, width))
    highest = lax.Precision.HIGHEST
    out_real = jnp.einsum(
        "abnej,eij->abnei", real_blocks, matrices[0], precision=highest
    ) - jnp.einsum("abnej,eij->abnei", imag_blocks, matrices[1], precision=highest)
    out_imag = jnp.einsum(
        "abnej,eij->abnei", imag_blocks, matrices[0], precision=highest
    ) + jnp.einsum("abnej,eij->abnei", real_blocks, matrices[1], precision=highest)
    return (out_real.reshape(shape_in), out_imag.reshape(shape_in))


def radial_half(channel_block, cosine, sine, matrices):
    real_part = channel_block[:, :, :, 0, :]
    imag_part = channel_block[:, :, :, 1, :]
    turned_real = real_part * cosine + imag_part * sine
    turned_imag = imag_part * cosine - real_part * sine
    out_real, out_imag = element_product(turned_real, turned_imag, matrices)
    return jnp.stack((out_real, out_imag), axis=3)


def halo_shards(
    start_amplitudes,
    coupling,
    block_pattern,
    counts,
    radial_terms,
    energy,
    potential,
    element_matrices,
):
    capacity = coupling.shape[2]
    orders = coupling.shape[1]
    tile_size = capacity // block_pattern.shape[1]
    pattern = jnp.repeat(jnp.repeat(block_pattern[0], tile_size, axis=0), tile_size, axis=2).astype(
        jnp.bfloat16
    )
    weights = (coupling[0] * pattern[None]).reshape(orders * capacity, 3 * capacity)
    live_rows = (
        (jnp.arange(capacity, dtype=jnp.int32) < counts[0])
        .astype(jnp.float32)
        .reshape(1, capacity, 1, 1)
    )
    columns = start_amplitudes.shape[3]
    block_points = radial_terms.shape[1]
    states = columns // (2 * block_points)
    points = potential.shape[0]
    blocks_all = points // block_points
    per_device = capacity // lax.axis_size("rad")
    first_row = lax.axis_index("rad") * per_device
    local_energy = lax.dynamic_slice_in_dim(energy[0], first_row, per_device)
    angles = local_energy[:, None] + potential[None, :]
    cosine = jnp.cos(angles)[None, :, None, :]
    sine = jnp.sin(angles)[None, :, None, :]
    radial_rows = jnp.broadcast_to(
        radial_terms[:, None, None, :], (orders, states, 2, block_points)
    ).reshape(orders, 1, columns)
    out_index = jnp.arange(columns, dtype=jnp.int32)
    out_part = out_index // block_points % 2
    in_index = out_index[:, None]
    swap_sign = jnp.where(
        (in_index == out_index[None, :] + block_points) & (out_part[None, :] == 0), 1.0, 0.0
    )
    swap_sign = swap_sign - jnp.where(
        (in_index == out_index[None, :] - block_points) & (out_part[None, :] == 1), 1.0, 0.0
    )
    swap_sign = swap_sign.astype(jnp.float32)

    def coupled_term(current):
        sent = current.astype(jnp.bfloat16)
        widened = extended(sent, (("sym", 0),), 1)
        product = jnp.dot(
            weights, widened.reshape(3 * capacity, columns), preferred_element_type=jnp.float32
        )
        product = product.reshape(orders, capacity, columns)
        coupled = jnp.sum(product * radial_rows, axis=0)
        return coupled.reshape(1, capacity, 1, columns) * live_rows

    def relay_block(amplitudes, repeats):
        channel_block = lax.all_to_all(amplitudes, "rad", split_axis=1, concat_axis=2, tiled=True)
        items = channel_block.shape[0]
        spread = channel_block.reshape(items, per_device, blocks_all, states, 2, block_points)
        spread = spread.transpose(0, 1, 3, 4, 2, 5).reshape(items, per_device, states, 2, points)
        for repeat_index in range(repeats):
            spread = radial_half(spread, cosine, sine, element_matrices)
        folded = spread.reshape(items, per_device, states, 2, blocks_all, block_points)
        moved = folded.transpose(0, 1, 4, 2, 3, 5).reshape(items, per_device, blocks_all, columns)
        return lax.all_to_all(moved, "rad", split_axis=2, concat_axis=1, tiled=True)

    amplitudes = start_amplitudes * live_rows
    amplitudes = relay_block(amplitudes, 1)
    for step_index in range(TIME_STEPS):
        first = step_length * coupled_term(amplitudes)
        second = step_length / 2.0 * coupled_term(first)
        third = step_length / 3.0 * coupled_term(second)
        even_sum = amplitudes - second
        odd_sum = (first - third).reshape(capacity, columns)
        turned = jnp.dot(
            odd_sum, swap_sign, precision=lax.Precision.HIGHEST, preferred_element_type=jnp.float32
        )
        amplitudes = even_sum + turned.reshape(1, capacity, 1, columns)
        amplitudes = relay_block(amplitudes, 1 if step_index + 1 == TIME_STEPS else 2)
    return amplitudes


f32 = jnp.float32
bf16 = jnp.bfloat16
f16 = jnp.float16
NT = (((1,), (1,)), ((), ()))


def halves(x):
    high = x.astype(bf16)
    return high, (x - high.astype(f32)).astype(bf16)


def split_dot(a, b):
    a0, a1 = halves(a)
    b0, b1 = halves(b)

    def mm(x, y):
        return lax.dot_general(x, y, NT, preferred_element_type=f32)

    return mm(a0, b0) + (mm(a0, b1) + mm(a1, b0))


def split_three(x):
    parts = []
    for _ in range(2):
        scaled = x * 8193.0
        high = scaled - (scaled - x)
        parts.append(high)
        x = (x - high) * 2048.0
    return parts + [x]


def pack_kernel(count_ref, start_ref, radial_ref, out_ref, turn):
    capacity, columns = start_ref.shape
    hosts, rows, width = out_ref.shape
    orders, block = radial_ref.shape
    states = columns // rows
    row = lax.broadcasted_iota(jnp.int32, (capacity, columns), 0)
    turned = jnp.where(row < count_ref[0], start_ref[...], 0.0).T
    turn[...] = jnp.zeros_like(turn)
    for index, part in enumerate(split_three(radial_ref[...])):
        turn[8 * index : 8 * index + orders, :block] = part
    radial = turn[...].T[:block]
    for host in range(hosts):
        state = host // (hosts // states)
        out_ref[host, :, :capacity] = turned[state * rows : (state + 1) * rows]
        for p in range(2):
            out_ref[host, p * block : (p + 1) * block, capacity:] = radial


def unpack_kernel(in_ref, out_ref):
    states, rows, capacity = in_ref.shape
    out_ref[...] = in_ref[...].reshape(states * rows, capacity).astype(f32).T


def steps_kernel(
    orders,
    block,
    info_ref,
    own_w,
    other_w,
    own_x,
    other_x,
    phase_ref,
    turn_ref,
    matrix_ref,
    out_ref,
    weights,
    current,
    following,
    total,
    factors,
    phases,
    one_half,
    two_half,
    sems,
):
    tiles = weights.shape[1]
    tile = weights.shape[3]
    capacity = tiles * tile
    columns = current.shape[1]
    width = columns // 2
    me = info_ref[0]
    part = info_ref[1]
    per_slot = tiles * 3 * tiles

    def fetch(a, i, b):
        k = 1 if a == b else (2 - 2 * me if a == 0 else 2 * me)
        source = own_w if a == 0 else other_w
        return pltpu.make_async_copy(
            source.at[:, k, i * tile : (i + 1) * tile, :],
            weights.at[a, i, :, :, b * capacity : (b + 1) * capacity],
            sems.at[a, i, b],
        )

    for a in range(2):
        for i in range(tiles):
            for b in range(2):
                fetch(a, i, b).start()

    m0 = matrix_ref[0]
    m1 = matrix_ref[1]
    cosine = turn_ref[0:1]
    sine = turn_ref[1:2]
    k0 = m0 * cosine + m1 * sine
    k1 = m1 * cosine - m0 * sine

    def store_pair(ref, real, imag):
        ref[:width, :width] = real
        ref[:width, width:] = -imag
        ref[width:, :width] = imag
        ref[width:, width:] = real

    store_pair(one_half, k0, k1)
    highest = lax.Precision.HIGHEST
    square = lambda x, y: jnp.dot(x, y, precision=highest, preferred_element_type=f32)
    store_pair(two_half, square(k0, k0) - square(k1, k1), square(k0, k1) + square(k1, k0))

    phases[...] = phase_ref[...].T

    def rotated(v, a, col):
        c = phases[:, 4 * a + col : 4 * a + col + 1]
        s = phases[:, 4 * a + col + 1 : 4 * a + col + 2]
        real, imag = v[:, :width], v[:, width:]
        return jnp.concatenate([real * c + imag * s, imag * c - real * s], axis=1)

    def begin(a, v):
        total[a * capacity : (a + 1) * capacity] = v
        current[a * capacity : (a + 1) * capacity] = v.astype(bf16)

    for a, x_ref in enumerate((own_x, other_x)):
        x = x_ref[...]
        blocks = x.shape[0] // (2 * block)
        pieces = [
            x[(2 * n + p) * block : (2 * n + p + 1) * block] for p in range(2) for n in range(blocks)
        ]
        turned = jnp.concatenate(pieces, axis=0).T
        begin(a, rotated(split_dot(turned[:capacity], one_half[...]), a, 0))
        if a == 0:
            for l in range(orders):
                high, middle, low = (
                    turned[capacity + 8 * n + l : capacity + 8 * n + l + 1] for n in range(3)
                )
                factors[l : l + 1] = high + (middle + low / 2048.0) / 2048.0

    def couple(factor, ready):
        radial = [factors[l : l + 1] * factor for l in range(orders)]
        for a in range(2):
            count = info_ref[2 + a]
            for i in range(tiles):
                if not ready:
                    for b in range(2):
                        fetch(a, i, b).wait()
                    for b in range(2):
                        k = 1 if a == b else (2 - 2 * me if a == 0 else 2 * me)
                        for j in range(tiles):
                            present = info_ref[4 + a * per_slot + (i * 3 + k) * tiles + j]
                            first = b * capacity + j * tile

                            @pl.when(present == 0)
                            def _():
                                weights[a, i, :, :, first : first + tile] = jnp.zeros(
                                    (orders, tile, tile), bf16
                                )

                w = weights[a, i].reshape(orders * tile, 2 * capacity)
                product = jnp.dot(w, current[...], preferred_element_type=f32)
                u = product[:tile] * radial[0]
                for l in range(1, orders):
                    u = u + product[l * tile : (l + 1) * tile] * radial[l]
                row = lax.broadcasted_iota(jnp.int32, u.shape, 0) + i * tile
                u = jnp.where(row < count, u, 0.0)
                term = jnp.concatenate([u[:, width:], -u[:, :width]], axis=1)
                first = a * capacity + i * tile
                total[first : first + tile] += term
                following[first : first + tile] = term.astype(bf16)

        current[...] = following[...]

    step_length_over = lambda k: jnp.where(
        k == 0, step_length, jnp.where(k == 1, step_length / 2.0, step_length / 3.0)
    )
    couple(step_length, False)

    def later(index, carry):
        k = lax.rem(index, 3)

        @pl.when(k == 0)
        def _():
            for a in range(2):
                v = total[a * capacity : (a + 1) * capacity]
                v = rotated(split_dot(v, two_half[...]), a, 2)
                total[a * capacity : (a + 1) * capacity] = v
                current[a * capacity : (a + 1) * capacity] = v.astype(bf16)

        couple(step_length_over(k), True)
        return carry

    lax.fori_loop(1, 3 * TIME_STEPS, later, 0)

    final = rotated(total[:capacity], 0, 0)
    pieces = out_ref.shape[0]
    spread = width // (block * pieces)
    for m in range(pieces):
        for p in range(2):
            first = pl.multiple_of(p * width + (m * spread + part) * block, block)
            two_half[(2 * m + p) * block : (2 * m + p + 1) * block] = one_half[pl.ds(first, block)]
    result = split_dot(two_half[: 2 * pieces * block], final)
    out_ref[...] = result.astype(bf16).reshape(out_ref.shape)


def pair_shards(
    start_amplitudes,
    coupling,
    block_pattern,
    counts,
    radial_terms,
    energy,
    potential,
    element_matrices,
):
    orders, capacity = coupling.shape[1:3]
    tiles = block_pattern.shape[1]
    tile = capacity // tiles
    columns = start_amplitudes.shape[3]
    block = radial_terms.shape[1]
    width = element_matrices.shape[2]
    elements = element_matrices.shape[1]
    states = columns // (2 * block)
    group = width // block
    spread = group // states
    rows = 2 * block
    vmem = pl.BlockSpec(memory_space=pltpu.VMEM)
    smem = pl.BlockSpec(memory_space=pltpu.SMEM)
    anywhere = pl.BlockSpec(memory_space=pl.ANY)
    swap = [(0, 1), (1, 0)]
    place = lax.axis_index("rad")
    me = lax.axis_index("sym")
    element = place // group

    other_coupling = lax.ppermute(coupling, "sym", swap)
    angle = energy[0]
    phase = jnp.stack([jnp.cos(angle), jnp.sin(angle), jnp.cos(2.0 * angle), jnp.sin(2.0 * angle)])
    integers = jnp.concatenate([counts, block_pattern.reshape(-1)]).astype(f32)
    padded = -(-integers.shape[0] // capacity) * capacity
    small = jnp.concatenate(
        [phase, jnp.pad(integers, (0, padded - integers.shape[0])).reshape(-1, capacity)]
    )
    other_small = lax.ppermute(small, "sym", swap)
    other_integers = other_small[4:].reshape(-1)[: integers.shape[0]].astype(jnp.int32)
    info = jnp.concatenate(
        [
            jnp.stack([me, place % spread, counts[0], other_integers[0]]).astype(jnp.int32),
            block_pattern.reshape(-1),
            other_integers[1:],
        ]
    )
    lanes = 128
    phases = jnp.concatenate(
        [phase, other_small[:4], jnp.zeros((lanes - 8, capacity), f32)]
    )
    radii = lax.dynamic_slice_in_dim(potential, element * width, width)
    turn = jnp.stack([jnp.cos(radii), jnp.sin(radii)])
    matrices = lax.dynamic_index_in_dim(element_matrices, element, 1, keepdims=False)

    packed = pl.pallas_call(
        pack_kernel,
        out_shape=jax.ShapeDtypeStruct((group, rows, capacity + lanes), f32),
        in_specs=[smem, vmem, vmem],
        out_specs=vmem,
        scratch_shapes=[pltpu.VMEM((lanes, lanes), f32)],
        compiler_params=pltpu.CompilerParams(vmem_limit_bytes=4 << 20),
        name="pack",
    )(counts, start_amplitudes.reshape(capacity, columns), radial_terms)
    wide = [[e * group + d for d in range(group)] for e in range(elements)]
    gathered = lax.all_to_all(
        packed.astype(f16), "rad", split_axis=0, concat_axis=0, tiled=True, axis_index_groups=wide
    ).reshape(group * rows, capacity + lanes)
    other_gathered = lax.ppermute(gathered, "sym", swap)

    def by_order(x):
        return x[0].transpose(0, 2, 1, 3)

    scratch = [
        pltpu.VMEM((2, tiles, orders, tile, 2 * capacity), bf16),
        pltpu.VMEM((2 * capacity, 2 * width), bf16),
        pltpu.VMEM((2 * capacity, 2 * width), bf16),
        pltpu.VMEM((2 * capacity, 2 * width), f32),
        pltpu.VMEM((8, 2 * width), f32),
        pltpu.VMEM((capacity, lanes), f32),
        pltpu.VMEM((2 * width, 2 * width), f32),
        pltpu.VMEM((2 * width, 2 * width), f32),
        pltpu.SemaphoreType.DMA((2, tiles, 2)),
    ]

    def body(*refs):
        steps_kernel(orders, block, *refs)

    result = pl.pallas_call(
        body,
        out_shape=jax.ShapeDtypeStruct((states, rows, capacity), bf16),
        in_specs=[smem, anywhere, anywhere, vmem, vmem, vmem, vmem, vmem],
        out_specs=vmem,
        scratch_shapes=scratch,
        compiler_params=pltpu.CompilerParams(vmem_limit_bytes=28 << 20),
        name="steps",
    )(
        info,
        by_order(coupling),
        by_order(other_coupling),
        gathered.astype(f32),
        other_gathered.astype(f32),
        phases,
        turn,
        matrices,
    )
    narrow = [
        [e * group + n * spread + d for n in range(states)]
        for e in range(elements)
        for d in range(spread)
    ]
    returned = lax.all_to_all(
        result, "rad", split_axis=0, concat_axis=0, tiled=True, axis_index_groups=narrow
    )
    out = pl.pallas_call(
        unpack_kernel,
        out_shape=jax.ShapeDtypeStruct((capacity, columns), f32),
        in_specs=[vmem],
        out_specs=vmem,
        compiler_params=pltpu.CompilerParams(vmem_limit_bytes=4 << 20),
        name="unpack",
    )(returned)
    return out.reshape(start_amplitudes.shape)


def solution(mesh):
    def program(*args):
        states = args[0].shape[3] // (2 * args[4].shape[1])
        group = args[7].shape[2] // args[4].shape[1]
        paired = mesh.shape["sym"] == 2 and group % states == 0
        return pair_shards(*args) if paired else halo_shards(*args)

    return jax.shard_map(
        program,
        mesh=mesh,
        in_specs=(
            P("sym", None, "rad", None),
            P("sym", None, None, None, None),
            P("sym", None, None, None),
            P("sym"),
            P(None, "rad"),
            P("sym", None),
            P(),
            P(),
        ),
        out_specs=P("sym", None, "rad", None),
        check_vma=False,
    )
```

```python
import jax
import jax.numpy as jnp
from jax import lax
from jax.experimental import pallas as pl
from jax.experimental.pallas import tpu as pltpu
from jax.sharding import PartitionSpec as P

TIME_STEPS = 2


step_length = 0.8


def extended(x, sides, width):
    for axis, dim in sides:
        size, length = (lax.axis_size(axis), x.shape[dim])
        up = [(i, (i + 1) % size) for i in range(size - 1)]
        down = [(j, i) for i, j in up]
        last = lax.slice_in_dim(x, length - width, length, axis=dim)
        initial = lax.slice_in_dim(x, 0, width, axis=dim)
        before = lax.ppermute(last, axis, up)
        after = lax.ppermute(initial, axis, down)
        x = jnp.concatenate([before, x, after], axis=dim)
    return x


def element_product(real_part, imag_part, matrices):
    shape_in = real_part.shape
    elements = matrices.shape[1]
    width = matrices.shape[2]
    real_blocks = real_part.reshape(shape_in[:-1] + (elements, width))
    imag_blocks = imag_part.reshape(shape_in[:-1] + (elements, width))
    highest = lax.Precision.HIGHEST
    out_real = jnp.einsum(
        "abnej,eij->abnei", real_blocks, matrices[0], precision=highest
    ) - jnp.einsum("abnej,eij->abnei", imag_blocks, matrices[1], precision=highest)
    out_imag = jnp.einsum(
        "abnej,eij->abnei", imag_blocks, matrices[0], precision=highest
    ) + jnp.einsum("abnej,eij->abnei", real_blocks, matrices[1], precision=highest)
    return (out_real.reshape(shape_in), out_imag.reshape(shape_in))


def radial_half(channel_block, cosine, sine, matrices):
    real_part = channel_block[:, :, :, 0, :]
    imag_part = channel_block[:, :, :, 1, :]
    turned_real = real_part * cosine + imag_part * sine
    turned_imag = imag_part * cosine - real_part * sine
    out_real, out_imag = element_product(turned_real, turned_imag, matrices)
    return jnp.stack((out_real, out_imag), axis=3)


def halo_shards(
    start_amplitudes,
    coupling,
    block_pattern,
    counts,
    radial_terms,
    energy,
    potential,
    element_matrices,
):
    capacity = coupling.shape[2]
    orders = coupling.shape[1]
    tile_size = capacity // block_pattern.shape[1]
    pattern = jnp.repeat(jnp.repeat(block_pattern[0], tile_size, axis=0), tile_size, axis=2).astype(
        jnp.bfloat16
    )
    weights = (coupling[0] * pattern[None]).reshape(orders * capacity, 3 * capacity)
    live_rows = (
        (jnp.arange(capacity, dtype=jnp.int32) < counts[0])
        .astype(jnp.float32)
        .reshape(1, capacity, 1, 1)
    )
    columns = start_amplitudes.shape[3]
    block_points = radial_terms.shape[1]
    states = columns // (2 * block_points)
    points = potential.shape[0]
    blocks_all = points // block_points
    per_device = capacity // lax.axis_size("rad")
    first_row = lax.axis_index("rad") * per_device
    local_energy = lax.dynamic_slice_in_dim(energy[0], first_row, per_device)
    angles = local_energy[:, None] + potential[None, :]
    cosine = jnp.cos(angles)[None, :, None, :]
    sine = jnp.sin(angles)[None, :, None, :]
    radial_rows = jnp.broadcast_to(
        radial_terms[:, None, None, :], (orders, states, 2, block_points)
    ).reshape(orders, 1, columns)
    out_index = jnp.arange(columns, dtype=jnp.int32)
    out_part = out_index // block_points % 2
    in_index = out_index[:, None]
    swap_sign = jnp.where(
        (in_index == out_index[None, :] + block_points) & (out_part[None, :] == 0), 1.0, 0.0
    )
    swap_sign = swap_sign - jnp.where(
        (in_index == out_index[None, :] - block_points) & (out_part[None, :] == 1), 1.0, 0.0
    )
    swap_sign = swap_sign.astype(jnp.float32)

    def coupled_term(current):
        sent = current.astype(jnp.bfloat16)
        widened = extended(sent, (("sym", 0),), 1)
        product = jnp.dot(
            weights, widened.reshape(3 * capacity, columns), preferred_element_type=jnp.float32
        )
        product = product.reshape(orders, capacity, columns)
        coupled = jnp.sum(product * radial_rows, axis=0)
        return coupled.reshape(1, capacity, 1, columns) * live_rows

    def relay_block(amplitudes, repeats):
        channel_block = lax.all_to_all(amplitudes, "rad", split_axis=1, concat_axis=2, tiled=True)
        items = channel_block.shape[0]
        spread = channel_block.reshape(items, per_device, blocks_all, states, 2, block_points)
        spread = spread.transpose(0, 1, 3, 4, 2, 5).reshape(items, per_device, states, 2, points)
        for repeat_index in range(repeats):
            spread = radial_half(spread, cosine, sine, element_matrices)
        folded = spread.reshape(items, per_device, states, 2, blocks_all, block_points)
        moved = folded.transpose(0, 1, 4, 2, 3, 5).reshape(items, per_device, blocks_all, columns)
        return lax.all_to_all(moved, "rad", split_axis=2, concat_axis=1, tiled=True)

    amplitudes = start_amplitudes * live_rows
    amplitudes = relay_block(amplitudes, 1)
    for step_index in range(TIME_STEPS):
        first = step_length * coupled_term(amplitudes)
        second = step_length / 2.0 * coupled_term(first)
        third = step_length / 3.0 * coupled_term(second)
        even_sum = amplitudes - second
        odd_sum = (first - third).reshape(capacity, columns)
        turned = jnp.dot(
            odd_sum, swap_sign, precision=lax.Precision.HIGHEST, preferred_element_type=jnp.float32
        )
        amplitudes = even_sum + turned.reshape(1, capacity, 1, columns)
        amplitudes = relay_block(amplitudes, 1 if step_index + 1 == TIME_STEPS else 2)
    return amplitudes


f32 = jnp.float32
bf16 = jnp.bfloat16
f16 = jnp.float16
NT = (((1,), (1,)), ((), ()))


def halves(x):
    high = x.astype(bf16)
    return high, (x - high.astype(f32)).astype(bf16)


def split_dot(a, b):
    def mm(x, y):
        return lax.dot_general(x, y, NT, preferred_element_type=f32)

    return mm(a[0], b[0]) + (mm(a[0], b[1]) + mm(a[1], b[0]))


def split_three(x):
    parts = []
    for _ in range(2):
        scaled = x * 8193.0
        high = scaled - (scaled - x)
        parts.append(high)
        x = (x - high) * 2048.0
    return parts + [x]


def pack_kernel(count_ref, start_hbm, radial_hbm, out_ref, turn, start_ref, radial_ref, sems):
    capacity, columns = start_ref.shape
    copies = [
        pltpu.make_async_copy(start_hbm, start_ref, sems.at[0]),
        pltpu.make_async_copy(radial_hbm, radial_ref, sems.at[1]),
    ]
    for copy in copies:
        copy.start()
    hosts, rows, width = out_ref.shape
    orders, block = radial_ref.shape
    states = columns // rows
    turn[...] = jnp.zeros_like(turn)
    for copy in copies:
        copy.wait()
    row = lax.broadcasted_iota(jnp.int32, (capacity, columns), 0)
    turned = jnp.where(row < count_ref[0], start_ref[...], 0.0).T
    for index, part in enumerate(split_three(radial_ref[...])):
        turn[8 * index : 8 * index + orders, :block] = part
    radial = turn[...].T[:block]
    for host in range(hosts):
        state = host // (hosts // states)
        out_ref[host, :, :capacity] = turned[state * rows : (state + 1) * rows]
        for p in range(2):
            out_ref[host, p * block : (p + 1) * block, capacity:] = radial


def unpack_kernel(in_ref, out_ref):
    states, rows, capacity = in_ref.shape
    out_ref[...] = in_ref[...].reshape(states * rows, capacity).astype(f32).T


def tables_kernel(angle_ref, radii_ref, matrix_ref, one_ref, two_ref, phase_ref, rows):
    width = matrix_ref.shape[1]
    m0 = matrix_ref[0]
    m1 = matrix_ref[1]
    cosine = jnp.cos(radii_ref[...])
    sine = jnp.sin(radii_ref[...])
    k0 = m0 * cosine + m1 * sine
    k1 = m1 * cosine - m0 * sine

    def store_pair(ref, real, imag):
        ref[:width, :width] = real
        ref[:width, width:] = -imag
        ref[width:, :width] = imag
        ref[width:, width:] = real

    def mm(x, y):
        return jnp.dot(x, y, precision=lax.Precision.HIGHEST, preferred_element_type=f32)

    store_pair(one_ref, k0, k1)
    store_pair(two_ref, mm(k0, k0) - mm(k1, k1), mm(k0, k1) + mm(k1, k0))
    angle = angle_ref[...]
    rows[...] = jnp.zeros_like(rows)
    for index, value in enumerate((jnp.cos(angle), jnp.sin(angle), jnp.cos(2.0 * angle), jnp.sin(2.0 * angle))):
        rows[2 * index : 2 * index + 2] = value
    phase_ref[...] = rows[...].T


def steps_kernel(
    orders,
    block,
    info_ref,
    own_w,
    other_w,
    own_x,
    other_x,
    one_half,
    two_half,
    phases,
    out_ref,
    weights,
    current,
    following,
    total,
    factors,
    selected,
    sems,
):
    tiles = weights.shape[1]
    tile = weights.shape[3]
    capacity = tiles * tile
    width = current.shape[1] // 2
    part = info_ref[0]
    me = info_ref[1]

    def order_of(a, b):
        return 1 if a == b else (2 - 2 * me if a == 0 else 2 * me)

    def fetch(a, i, b):
        return pltpu.make_async_copy(
            (other_w if a else own_w).at[:, order_of(a, b), i * tile : (i + 1) * tile, :],
            weights.at[a, i, :, :, b * capacity : (b + 1) * capacity],
            sems.at[a, i, b],
        )

    def settle(a, i):
        for b in range(2):
            fetch(a, i, b).wait()
            for j in range(tiles):
                entry = ((a * tiles + i) * 3 + order_of(a, b)) * tiles + j
                first = b * capacity + j * tile

                @pl.when(info_ref[4 + entry] == 0)
                def _():
                    weights[a, i, :, :, first : first + tile] = jnp.zeros((orders, tile, tile), bf16)

    for a in range(2):
        for i in range(tiles):
            for b in range(2):
                fetch(a, i, b).start()

    def rotated(v, a, first, col):
        rows = slice(first, first + v.shape[0])
        c = phases[rows, 4 * col + a : 4 * col + a + 1]
        s = phases[rows, 4 * col + 2 + a : 4 * col + 3 + a]
        real, imag = v[:, :width], v[:, width:]
        return jnp.concatenate([real * c + imag * s, imag * c - real * s], axis=1)

    def begin(a, first, v):
        total[a * capacity + first : a * capacity + first + v.shape[0]] = v
        current[a * capacity + first : a * capacity + first + v.shape[0]] = v.astype(bf16)

    matrix = halves(one_half[...])
    for a, x_ref in enumerate((own_x, other_x)):
        blocks = x_ref.shape[0] // (2 * block)
        for i in range(tiles + (a == 0)):
            first = i * tile
            pieces = [
                x_ref[(2 * n + p) * block : (2 * n + p + 1) * block, first : first + tile]
                for p in range(2)
                for n in range(blocks)
            ]
            turned = jnp.concatenate(pieces, axis=0).T
            if i < tiles:
                begin(a, first, rotated(split_dot(halves(turned), matrix), a, first, 0))
            else:
                for l in range(orders):
                    high, middle, low = (turned[8 * n + l : 8 * n + l + 1] for n in range(3))
                    factors[l : l + 1] = high + (middle + low / 2048.0) / 2048.0

    def couple(factor, ready):
        radial = [factors[l : l + 1] * factor for l in range(orders)]
        for a in range(2):
            count = info_ref[2 + a]
            for i in range(tiles):
                if not ready:
                    settle(a, i)
                w = weights[a, i].reshape(orders * tile, 2 * capacity)
                product = jnp.dot(w, current[...], preferred_element_type=f32)
                u = product[:tile] * radial[0]
                for l in range(1, orders):
                    u = u + product[l * tile : (l + 1) * tile] * radial[l]
                row = lax.broadcasted_iota(jnp.int32, u.shape, 0) + i * tile
                u = jnp.where(row < count, u, 0.0)
                term = jnp.concatenate([u[:, width:], -u[:, :width]], axis=1)
                first = a * capacity + i * tile
                total[first : first + tile] += term
                following[first : first + tile] = term.astype(bf16)
        current[...] = following[...]

    def run(index, carry):
        k = lax.rem(index, 3)

        @pl.when(k == 0)
        def _():
            square = halves(two_half[...])
            for a in range(2):
                for i in range(tiles):
                    first = i * tile
                    v = halves(total[a * capacity + first : a * capacity + first + tile])
                    begin(a, first, rotated(split_dot(v, square), a, first, 1))

        factor = jnp.where(k == 1, step_length / 2.0, step_length / 3.0)
        couple(jnp.where(k == 0, step_length, factor), True)
        return carry

    couple(step_length, False)
    lax.fori_loop(1, 3 * TIME_STEPS, run, 0)

    pieces = out_ref.shape[0]
    spread = width // (block * pieces)
    for m in range(pieces):
        for p in range(2):
            first = pl.multiple_of(p * width + (m * spread + part) * block, block)
            selected[(2 * m + p) * block : (2 * m + p + 1) * block] = one_half[pl.ds(first, block)]
    matrix = halves(selected[...])
    for i in range(tiles):
        first = i * tile
        v = halves(rotated(total[first : first + tile], 0, first, 0))
        result = split_dot(matrix, v).astype(bf16)
        for m in range(pieces):
            out_ref[m, :, first : first + tile] = result[2 * m * block : 2 * (m + 1) * block]


def pair_shards(
    start_amplitudes,
    coupling,
    block_pattern,
    counts,
    radial_terms,
    energy,
    potential,
    element_matrices,
):
    orders, capacity = coupling.shape[1:3]
    tiles = block_pattern.shape[1]
    tile = capacity // tiles
    columns = start_amplitudes.shape[3]
    block = radial_terms.shape[1]
    width = element_matrices.shape[2]
    elements = element_matrices.shape[1]
    states = columns // (2 * block)
    group = width // block
    spread = group // states
    rows = 2 * block
    vmem = pl.BlockSpec(memory_space=pltpu.VMEM)
    smem = pl.BlockSpec(memory_space=pltpu.SMEM)
    hbm = pl.BlockSpec(memory_space=pltpu.HBM)
    swap = [(0, 1), (1, 0)]
    place = lax.axis_index("rad")
    me = lax.axis_index("sym")
    element = place // group

    lanes = 128
    integers = jnp.concatenate([counts, block_pattern.reshape(-1)]).astype(f32)
    padded = -(-integers.shape[0] // capacity) * capacity
    small = jnp.concatenate(
        [energy, jnp.pad(integers, (0, padded - integers.shape[0])).reshape(-1, capacity)]
    )
    other_small = lax.ppermute(small, "sym", swap)
    other_integers = other_small[1:].reshape(-1)[: integers.shape[0]].astype(jnp.int32)
    other_coupling = lax.ppermute(coupling, "sym", swap)
    radii = lax.dynamic_slice_in_dim(potential, element * width, width)
    matrices = lax.dynamic_index_in_dim(element_matrices, element, 1, keepdims=False)
    info = jnp.concatenate(
        [
            jnp.stack([place % spread, me, counts[0], other_integers[0]]).astype(jnp.int32),
            block_pattern.reshape(-1),
            other_integers[1:],
        ]
    )
    square = jax.ShapeDtypeStruct((2 * width, 2 * width), f32)
    one_half, two_half, phases = pl.pallas_call(
        tables_kernel,
        out_shape=(square, square, jax.ShapeDtypeStruct((capacity, lanes), f32)),
        in_specs=[vmem] * 3,
        out_specs=(vmem,) * 3,
        scratch_shapes=[pltpu.VMEM((lanes, capacity), f32)],
        compiler_params=pltpu.CompilerParams(vmem_limit_bytes=6 << 20),
        name="tables",
    )(jnp.concatenate([energy, other_small[:1]]), radii[None], matrices)

    packed = pl.pallas_call(
        pack_kernel,
        out_shape=jax.ShapeDtypeStruct((group, rows, capacity + lanes), f32),
        in_specs=[smem, hbm, hbm],
        out_specs=vmem,
        scratch_shapes=[
            pltpu.VMEM((lanes, lanes), f32),
            pltpu.VMEM((capacity, columns), f32),
            pltpu.VMEM((orders, block), f32),
            pltpu.SemaphoreType.DMA((2,)),
        ],
        compiler_params=pltpu.CompilerParams(vmem_limit_bytes=4 << 20),
        name="pack",
    )(
        counts,
        pltpu.with_memory_space_constraint(start_amplitudes.reshape(capacity, columns), pltpu.HBM),
        pltpu.with_memory_space_constraint(radial_terms, pltpu.HBM),
    )
    wide = [[e * group + d for d in range(group)] for e in range(elements)]
    gathered = lax.all_to_all(
        packed.astype(f16), "rad", split_axis=0, concat_axis=0, tiled=True, axis_index_groups=wide
    ).reshape(group * rows, capacity + lanes)
    other_gathered = lax.ppermute(gathered, "sym", swap)

    def by_order(x):
        return pltpu.with_memory_space_constraint(x[0].transpose(0, 2, 1, 3), pltpu.HBM)

    def body(*refs):
        steps_kernel(orders, block, *refs)

    result = pl.pallas_call(
        body,
        out_shape=jax.ShapeDtypeStruct((states, rows, capacity), bf16),
        in_specs=[smem, hbm, hbm] + [vmem] * 5,
        out_specs=vmem,
        scratch_shapes=[
            pltpu.VMEM((2, tiles, orders, tile, 2 * capacity), bf16),
            pltpu.VMEM((2 * capacity, 2 * width), bf16),
            pltpu.VMEM((2 * capacity, 2 * width), bf16),
            pltpu.VMEM((2 * capacity, 2 * width), f32),
            pltpu.VMEM((8, 2 * width), f32),
            pltpu.VMEM((states * rows, 2 * width), f32),
            pltpu.SemaphoreType.DMA((2, tiles, 2)),
        ],
        compiler_params=pltpu.CompilerParams(vmem_limit_bytes=28 << 20),
        name="steps",
    )(
        info,
        by_order(coupling),
        by_order(other_coupling),
        gathered.astype(f32),
        other_gathered.astype(f32),
        one_half,
        two_half,
        phases,
    )
    narrow = [
        [e * group + n * spread + d for n in range(states)]
        for e in range(elements)
        for d in range(spread)
    ]
    returned = lax.all_to_all(
        result, "rad", split_axis=0, concat_axis=0, tiled=True, axis_index_groups=narrow
    )
    out = pl.pallas_call(
        unpack_kernel,
        out_shape=jax.ShapeDtypeStruct((capacity, columns), f32),
        in_specs=[vmem],
        out_specs=vmem,
        compiler_params=pltpu.CompilerParams(vmem_limit_bytes=4 << 20),
        name="unpack",
    )(returned)
    return out.reshape(start_amplitudes.shape)


def solution(mesh):
    def program(*args):
        states = args[0].shape[3] // (2 * args[4].shape[1])
        group = args[7].shape[2] // args[4].shape[1]
        paired = mesh.shape["sym"] == 2 and group % states == 0
        return pair_shards(*args) if paired else halo_shards(*args)

    return jax.shard_map(
        program,
        mesh=mesh,
        in_specs=(
            P("sym", None, "rad", None),
            P("sym", None, None, None, None),
            P("sym", None, None, None),
            P("sym"),
            P(None, "rad"),
            P("sym", None),
            P(),
            P(),
        ),
        out_specs=P("sym", None, "rad", None),
        check_vma=False,
    )
```

```python
import jax
import jax.numpy as jnp
from jax import lax
from jax.experimental import pallas as pl
from jax.experimental.pallas import tpu as pltpu
from jax.sharding import PartitionSpec as P

TIME_STEPS = 2


step_length = 0.8


def extended(x, sides, width):
    for axis, dim in sides:
        size, length = (lax.axis_size(axis), x.shape[dim])
        up = [(i, (i + 1) % size) for i in range(size - 1)]
        down = [(j, i) for i, j in up]
        last = lax.slice_in_dim(x, length - width, length, axis=dim)
        initial = lax.slice_in_dim(x, 0, width, axis=dim)
        before = lax.ppermute(last, axis, up)
        after = lax.ppermute(initial, axis, down)
        x = jnp.concatenate([before, x, after], axis=dim)
    return x


def element_product(real_part, imag_part, matrices):
    shape_in = real_part.shape
    elements = matrices.shape[1]
    width = matrices.shape[2]
    real_blocks = real_part.reshape(shape_in[:-1] + (elements, width))
    imag_blocks = imag_part.reshape(shape_in[:-1] + (elements, width))
    highest = lax.Precision.HIGHEST
    out_real = jnp.einsum(
        "abnej,eij->abnei", real_blocks, matrices[0], precision=highest
    ) - jnp.einsum("abnej,eij->abnei", imag_blocks, matrices[1], precision=highest)
    out_imag = jnp.einsum(
        "abnej,eij->abnei", imag_blocks, matrices[0], precision=highest
    ) + jnp.einsum("abnej,eij->abnei", real_blocks, matrices[1], precision=highest)
    return (out_real.reshape(shape_in), out_imag.reshape(shape_in))


def radial_half(channel_block, cosine, sine, matrices):
    real_part = channel_block[:, :, :, 0, :]
    imag_part = channel_block[:, :, :, 1, :]
    turned_real = real_part * cosine + imag_part * sine
    turned_imag = imag_part * cosine - real_part * sine
    out_real, out_imag = element_product(turned_real, turned_imag, matrices)
    return jnp.stack((out_real, out_imag), axis=3)


def halo_shards(
    start_amplitudes,
    coupling,
    block_pattern,
    counts,
    radial_terms,
    energy,
    potential,
    element_matrices,
):
    capacity = coupling.shape[2]
    orders = coupling.shape[1]
    tile_size = capacity // block_pattern.shape[1]
    pattern = jnp.repeat(jnp.repeat(block_pattern[0], tile_size, axis=0), tile_size, axis=2).astype(
        jnp.bfloat16
    )
    weights = (coupling[0] * pattern[None]).reshape(orders * capacity, 3 * capacity)
    live_rows = (
        (jnp.arange(capacity, dtype=jnp.int32) < counts[0])
        .astype(jnp.float32)
        .reshape(1, capacity, 1, 1)
    )
    columns = start_amplitudes.shape[3]
    block_points = radial_terms.shape[1]
    states = columns // (2 * block_points)
    points = potential.shape[0]
    blocks_all = points // block_points
    per_device = capacity // lax.axis_size("rad")
    first_row = lax.axis_index("rad") * per_device
    local_energy = lax.dynamic_slice_in_dim(energy[0], first_row, per_device)
    angles = local_energy[:, None] + potential[None, :]
    cosine = jnp.cos(angles)[None, :, None, :]
    sine = jnp.sin(angles)[None, :, None, :]
    radial_rows = jnp.broadcast_to(
        radial_terms[:, None, None, :], (orders, states, 2, block_points)
    ).reshape(orders, 1, columns)
    out_index = jnp.arange(columns, dtype=jnp.int32)
    out_part = out_index // block_points % 2
    in_index = out_index[:, None]
    swap_sign = jnp.where(
        (in_index == out_index[None, :] + block_points) & (out_part[None, :] == 0), 1.0, 0.0
    )
    swap_sign = swap_sign - jnp.where(
        (in_index == out_index[None, :] - block_points) & (out_part[None, :] == 1), 1.0, 0.0
    )
    swap_sign = swap_sign.astype(jnp.float32)

    def coupled_term(current):
        sent = current.astype(jnp.bfloat16)
        widened = extended(sent, (("sym", 0),), 1)
        product = jnp.dot(
            weights, widened.reshape(3 * capacity, columns), preferred_element_type=jnp.float32
        )
        product = product.reshape(orders, capacity, columns)
        coupled = jnp.sum(product * radial_rows, axis=0)
        return coupled.reshape(1, capacity, 1, columns) * live_rows

    def relay_block(amplitudes, repeats):
        channel_block = lax.all_to_all(amplitudes, "rad", split_axis=1, concat_axis=2, tiled=True)
        items = channel_block.shape[0]
        spread = channel_block.reshape(items, per_device, blocks_all, states, 2, block_points)
        spread = spread.transpose(0, 1, 3, 4, 2, 5).reshape(items, per_device, states, 2, points)
        for repeat_index in range(repeats):
            spread = radial_half(spread, cosine, sine, element_matrices)
        folded = spread.reshape(items, per_device, states, 2, blocks_all, block_points)
        moved = folded.transpose(0, 1, 4, 2, 3, 5).reshape(items, per_device, blocks_all, columns)
        return lax.all_to_all(moved, "rad", split_axis=2, concat_axis=1, tiled=True)

    amplitudes = start_amplitudes * live_rows
    amplitudes = relay_block(amplitudes, 1)
    for step_index in range(TIME_STEPS):
        first = step_length * coupled_term(amplitudes)
        second = step_length / 2.0 * coupled_term(first)
        third = step_length / 3.0 * coupled_term(second)
        even_sum = amplitudes - second
        odd_sum = (first - third).reshape(capacity, columns)
        turned = jnp.dot(
            odd_sum, swap_sign, precision=lax.Precision.HIGHEST, preferred_element_type=jnp.float32
        )
        amplitudes = even_sum + turned.reshape(1, capacity, 1, columns)
        amplitudes = relay_block(amplitudes, 1 if step_index + 1 == TIME_STEPS else 2)
    return amplitudes


f32 = jnp.float32
bf16 = jnp.bfloat16
f16 = jnp.float16


def halves(x):
    high = x.astype(bf16)
    return high, (x - high.astype(f32)).astype(bf16)


def wide_halves(x):
    high, low = halves(x)
    return jnp.concatenate([high, low, high], axis=1)


def stacked_halves(x):
    high, low = halves(x)
    return jnp.concatenate([high, high, low], axis=0)


def split_three(x):
    parts = []
    for _ in range(2):
        scaled = x * 8193.0
        high = scaled - (scaled - x)
        parts.append(high)
        x = (x - high) * 2048.0
    return parts + [x]


def pack_kernel(count_ref, start_hbm, radial_hbm, out_ref, turn, start_ref, radial_ref, sems):
    capacity, columns = start_ref.shape
    copies = [
        pltpu.make_async_copy(start_hbm, start_ref, sems.at[0]),
        pltpu.make_async_copy(radial_hbm, radial_ref, sems.at[1]),
    ]
    for copy in copies:
        copy.start()
    hosts, rows, width = out_ref.shape
    orders, block = radial_ref.shape
    states = columns // rows
    turn[...] = jnp.zeros_like(turn)
    for copy in copies:
        copy.wait()
    row = lax.broadcasted_iota(jnp.int32, (capacity, columns), 0)
    turned = jnp.where(row < count_ref[0], start_ref[...], 0.0).T
    for index, part in enumerate(split_three(radial_ref[...])):
        turn[8 * index : 8 * index + orders, :block] = part
    radial = turn[...].T[:block]
    for host in range(hosts):
        state = host // (hosts // states)
        out_ref[host, :, :capacity] = turned[state * rows : (state + 1) * rows]
        for p in range(2):
            out_ref[host, p * block : (p + 1) * block, capacity:] = radial


def unpack_kernel(in_ref, out_ref):
    states, rows, capacity = in_ref.shape
    out_ref[...] = in_ref[...].reshape(states * rows, capacity).astype(f32).T


def tables_kernel(angle_ref, radii_ref, matrix_ref, one_ref, two_ref, phase_ref, rows):
    width = matrix_ref.shape[1]
    m0 = matrix_ref[0]
    m1 = matrix_ref[1]
    cosine = jnp.cos(radii_ref[...])
    sine = jnp.sin(radii_ref[...])
    k0 = m0 * cosine + m1 * sine
    k1 = m1 * cosine - m0 * sine

    def store_pair(ref, real, imag):
        real, imag = real.T, imag.T
        upper = jnp.concatenate([real, imag], axis=1)
        lower = jnp.concatenate([-imag, real], axis=1)
        ref[...] = stacked_halves(jnp.concatenate([upper, lower], axis=0))

    def mm(x, y):
        return jnp.dot(x, y, precision=lax.Precision.HIGHEST, preferred_element_type=f32)

    store_pair(one_ref, k0, k1)
    store_pair(two_ref, mm(k0, k0) - mm(k1, k1), mm(k0, k1) + mm(k1, k0))
    angle = angle_ref[...]
    rows[...] = jnp.zeros_like(rows)
    for index, value in enumerate((jnp.cos(angle), jnp.sin(angle), jnp.cos(2.0 * angle), jnp.sin(2.0 * angle))):
        rows[2 * index : 2 * index + 2] = value
    phase_ref[...] = rows[...].T


def steps_kernel(
    orders,
    block,
    info_ref,
    own_w,
    other_w,
    own_x,
    other_x,
    one_half,
    two_half,
    phases,
    out_ref,
    weights,
    current,
    following,
    total,
    factors,
    selected,
    sems,
):
    tiles = weights.shape[1]
    tile = weights.shape[3]
    capacity = tiles * tile
    width = current.shape[1] // 2
    part = info_ref[0]
    me = info_ref[1]

    def order_of(a, b):
        return 1 if a == b else (2 - 2 * me if a == 0 else 2 * me)

    def fetch(a, i, b):
        return pltpu.make_async_copy(
            (other_w if a else own_w).at[:, order_of(a, b), i * tile : (i + 1) * tile, :],
            weights.at[a, i, :, :, b * capacity : (b + 1) * capacity],
            sems.at[a, i, b],
        )

    def settle(a, i):
        for b in range(2):
            fetch(a, i, b).wait()
            for j in range(tiles):
                entry = ((a * tiles + i) * 3 + order_of(a, b)) * tiles + j
                first = b * capacity + j * tile

                @pl.when(info_ref[4 + entry] == 0)
                def _():
                    weights[a, i, :, :, first : first + tile] = jnp.zeros((orders, tile, tile), bf16)

    for a in range(2):
        for i in range(tiles):
            for b in range(2):
                fetch(a, i, b).start()

    def rotated(v, a, first, col):
        rows = slice(first, first + v.shape[0])
        c = phases[rows, 4 * col + a : 4 * col + a + 1]
        s = phases[rows, 4 * col + 2 + a : 4 * col + 3 + a]
        real, imag = v[:, :width], v[:, width:]
        return jnp.concatenate([real * c + imag * s, imag * c - real * s], axis=1)

    def begin(a, first, v):
        total[a * capacity + first : a * capacity + first + v.shape[0]] = v
        current[a * capacity + first : a * capacity + first + v.shape[0]] = v.astype(bf16)

    for a, x_ref in enumerate((own_x, other_x)):
        blocks = x_ref.shape[0] // (2 * block)
        pieces = [
            x_ref[(2 * n + p) * block : (2 * n + p + 1) * block]
            for p in range(2)
            for n in range(blocks)
        ]
        turned = jnp.concatenate(pieces, axis=0).T
        v = jnp.dot(wide_halves(turned[:capacity]), one_half[...], preferred_element_type=f32)
        begin(a, 0, rotated(v, a, 0, 0))
        if a == 0:
            for l in range(orders):
                high, middle, low = (
                    turned[capacity + 8 * n + l : capacity + 8 * n + l + 1] for n in range(3)
                )
                factors[l : l + 1] = high + (middle + low / 2048.0) / 2048.0
    for a in range(2):
        for i in range(tiles):
            settle(a, i)

    def couple(factor):
        radial = [factors[l : l + 1] * factor for l in range(orders)]
        for a in range(2):
            count = info_ref[2 + a]
            for i in range(tiles):
                w = weights[a, i].reshape(orders * tile, 2 * capacity)
                product = jnp.dot(w, current[...], preferred_element_type=f32)
                u = product[:tile] * radial[0]
                for l in range(1, orders):
                    u = u + product[l * tile : (l + 1) * tile] * radial[l]
                row = lax.broadcasted_iota(jnp.int32, u.shape, 0) + i * tile
                u = jnp.where(row < count, u, 0.0)
                term = jnp.concatenate([u[:, width:], -u[:, :width]], axis=1)
                first = a * capacity + i * tile
                total[first : first + tile] += term
                following[first : first + tile] = term.astype(bf16)
        current[...] = following[...]

    def run(index, carry):
        k = lax.rem(index, 3)

        @pl.when(jnp.logical_and(k == 0, index > 0))
        def _():
            high, low = halves(total[...])
            current[...] = high
            following[...] = low
            for a in range(2):
                rows = slice(a * capacity, (a + 1) * capacity)
                high = current[rows]
                v = jnp.dot(
                    jnp.concatenate([high, following[rows], high], axis=1),
                    two_half[...],
                    preferred_element_type=f32,
                )
                begin(a, 0, rotated(v, a, 0, 1))

        factor = jnp.where(k == 1, step_length / 2.0, step_length / 3.0)
        couple(jnp.where(k == 0, step_length, factor))
        return carry

    lax.fori_loop(0, 3 * TIME_STEPS, run, 0)

    pieces = out_ref.shape[0]
    spread = width // (block * pieces)
    v = wide_halves(rotated(total[:capacity], 0, 0, 0))
    selected[...] = jnp.dot(v, one_half[...], preferred_element_type=f32).T
    for m in range(pieces):
        for p in range(2):
            first = pl.multiple_of(p * width + (m * spread + part) * block, block)
            out_ref[m, p * block : (p + 1) * block] = selected[pl.ds(first, block)].astype(bf16)


def pair_shards(
    start_amplitudes,
    coupling,
    block_pattern,
    counts,
    radial_terms,
    energy,
    potential,
    element_matrices,
):
    orders, capacity = coupling.shape[1:3]
    tiles = block_pattern.shape[1]
    tile = capacity // tiles
    columns = start_amplitudes.shape[3]
    block = radial_terms.shape[1]
    width = element_matrices.shape[2]
    elements = element_matrices.shape[1]
    states = columns // (2 * block)
    group = width // block
    spread = group // states
    rows = 2 * block
    vmem = pl.BlockSpec(memory_space=pltpu.VMEM)
    smem = pl.BlockSpec(memory_space=pltpu.SMEM)
    hbm = pl.BlockSpec(memory_space=pltpu.HBM)
    swap = [(0, 1), (1, 0)]
    place = lax.axis_index("rad")
    me = lax.axis_index("sym")
    element = place // group

    lanes = 128
    integers = jnp.concatenate([counts, block_pattern.reshape(-1)]).astype(f32)
    padded = -(-integers.shape[0] // capacity) * capacity
    small = jnp.concatenate(
        [energy, jnp.pad(integers, (0, padded - integers.shape[0])).reshape(-1, capacity)]
    )
    other_small = lax.ppermute(small, "sym", swap)
    other_integers = other_small[1:].reshape(-1)[: integers.shape[0]].astype(jnp.int32)
    other_coupling = lax.ppermute(coupling, "sym", swap)
    radii = lax.dynamic_slice_in_dim(potential, element * width, width)
    matrices = lax.dynamic_index_in_dim(element_matrices, element, 1, keepdims=False)
    info = jnp.concatenate(
        [
            jnp.stack([place % spread, me, counts[0], other_integers[0]]).astype(jnp.int32),
            block_pattern.reshape(-1),
            other_integers[1:],
        ]
    )
    square = jax.ShapeDtypeStruct((6 * width, 2 * width), bf16)
    one_half, two_half, phases = pl.pallas_call(
        tables_kernel,
        out_shape=(square, square, jax.ShapeDtypeStruct((capacity, lanes), f32)),
        in_specs=[vmem] * 3,
        out_specs=(vmem,) * 3,
        scratch_shapes=[pltpu.VMEM((lanes, capacity), f32)],
        compiler_params=pltpu.CompilerParams(vmem_limit_bytes=6 << 20),
        name="tables",
    )(jnp.concatenate([energy, other_small[:1]]), radii[None], matrices)

    packed = pl.pallas_call(
        pack_kernel,
        out_shape=jax.ShapeDtypeStruct((group, rows, capacity + lanes), f32),
        in_specs=[smem, hbm, hbm],
        out_specs=vmem,
        scratch_shapes=[
            pltpu.VMEM((lanes, lanes), f32),
            pltpu.VMEM((capacity, columns), f32),
            pltpu.VMEM((orders, block), f32),
            pltpu.SemaphoreType.DMA((2,)),
        ],
        compiler_params=pltpu.CompilerParams(vmem_limit_bytes=4 << 20),
        name="pack",
    )(
        counts,
        pltpu.with_memory_space_constraint(start_amplitudes.reshape(capacity, columns), pltpu.HBM),
        pltpu.with_memory_space_constraint(radial_terms, pltpu.HBM),
    )
    wide = [[e * group + d for d in range(group)] for e in range(elements)]
    gathered = lax.all_to_all(
        packed.astype(f16), "rad", split_axis=0, concat_axis=0, tiled=True, axis_index_groups=wide
    ).reshape(group * rows, capacity + lanes)
    other_gathered = lax.ppermute(gathered, "sym", swap)

    def by_order(x):
        return pltpu.with_memory_space_constraint(x[0].transpose(0, 2, 1, 3), pltpu.HBM)

    def body(*refs):
        steps_kernel(orders, block, *refs)

    result = pl.pallas_call(
        body,
        out_shape=jax.ShapeDtypeStruct((states, rows, capacity), bf16),
        in_specs=[smem, hbm, hbm] + [vmem] * 5,
        out_specs=vmem,
        scratch_shapes=[
            pltpu.VMEM((2, tiles, orders, tile, 2 * capacity), bf16),
            pltpu.VMEM((2 * capacity, 2 * width), bf16),
            pltpu.VMEM((2 * capacity, 2 * width), bf16),
            pltpu.VMEM((2 * capacity, 2 * width), f32),
            pltpu.VMEM((8, 2 * width), f32),
            pltpu.VMEM((2 * width, capacity), f32),
            pltpu.SemaphoreType.DMA((2, tiles, 2)),
        ],
        compiler_params=pltpu.CompilerParams(vmem_limit_bytes=28 << 20),
        name="steps",
    )(
        info,
        by_order(coupling),
        by_order(other_coupling),
        gathered.astype(f32),
        other_gathered.astype(f32),
        one_half,
        two_half,
        phases,
    )
    narrow = [
        [e * group + n * spread + d for n in range(states)]
        for e in range(elements)
        for d in range(spread)
    ]
    returned = lax.all_to_all(
        result, "rad", split_axis=0, concat_axis=0, tiled=True, axis_index_groups=narrow
    )
    out = pl.pallas_call(
        unpack_kernel,
        out_shape=jax.ShapeDtypeStruct((capacity, columns), f32),
        in_specs=[vmem],
        out_specs=vmem,
        compiler_params=pltpu.CompilerParams(vmem_limit_bytes=4 << 20),
        name="unpack",
    )(returned)
    return out.reshape(start_amplitudes.shape)


def solution(mesh):
    def program(*args):
        states = args[0].shape[3] // (2 * args[4].shape[1])
        group = args[7].shape[2] // args[4].shape[1]
        paired = mesh.shape["sym"] == 2 and group % states == 0
        return pair_shards(*args) if paired else halo_shards(*args)

    return jax.shard_map(
        program,
        mesh=mesh,
        in_specs=(
            P("sym", None, "rad", None),
            P("sym", None, None, None, None),
            P("sym", None, None, None),
            P("sym"),
            P(None, "rad"),
            P("sym", None),
            P(),
            P(),
        ),
        out_specs=P("sym", None, "rad", None),
        check_vma=False,
    )
```

```python
import functools

import jax
import jax.numpy as jnp
from jax import lax
from jax.experimental import pallas as pl
from jax.experimental.pallas import tpu as pltpu
from jax.sharding import PartitionSpec as P

TIME_STEPS = 2


step_length = 0.8


def extended(x, sides, width):
    for axis, dim in sides:
        size, length = (lax.axis_size(axis), x.shape[dim])
        up = [(i, (i + 1) % size) for i in range(size - 1)]
        down = [(j, i) for i, j in up]
        last = lax.slice_in_dim(x, length - width, length, axis=dim)
        initial = lax.slice_in_dim(x, 0, width, axis=dim)
        before = lax.ppermute(last, axis, up)
        after = lax.ppermute(initial, axis, down)
        x = jnp.concatenate([before, x, after], axis=dim)
    return x


def element_product(real_part, imag_part, matrices):
    shape_in = real_part.shape
    elements = matrices.shape[1]
    width = matrices.shape[2]
    real_blocks = real_part.reshape(shape_in[:-1] + (elements, width))
    imag_blocks = imag_part.reshape(shape_in[:-1] + (elements, width))
    highest = lax.Precision.HIGHEST
    out_real = jnp.einsum(
        "abnej,eij->abnei", real_blocks, matrices[0], precision=highest
    ) - jnp.einsum("abnej,eij->abnei", imag_blocks, matrices[1], precision=highest)
    out_imag = jnp.einsum(
        "abnej,eij->abnei", imag_blocks, matrices[0], precision=highest
    ) + jnp.einsum("abnej,eij->abnei", real_blocks, matrices[1], precision=highest)
    return (out_real.reshape(shape_in), out_imag.reshape(shape_in))


def radial_half(channel_block, cosine, sine, matrices):
    real_part = channel_block[:, :, :, 0, :]
    imag_part = channel_block[:, :, :, 1, :]
    turned_real = real_part * cosine + imag_part * sine
    turned_imag = imag_part * cosine - real_part * sine
    out_real, out_imag = element_product(turned_real, turned_imag, matrices)
    return jnp.stack((out_real, out_imag), axis=3)


def halo_shards(
    start_amplitudes,
    coupling,
    block_pattern,
    counts,
    radial_terms,
    energy,
    potential,
    element_matrices,
):
    capacity = coupling.shape[2]
    orders = coupling.shape[1]
    tile_size = capacity // block_pattern.shape[1]
    pattern = jnp.repeat(jnp.repeat(block_pattern[0], tile_size, axis=0), tile_size, axis=2).astype(
        jnp.bfloat16
    )
    weights = (coupling[0] * pattern[None]).reshape(orders * capacity, 3 * capacity)
    live_rows = (
        (jnp.arange(capacity, dtype=jnp.int32) < counts[0])
        .astype(jnp.float32)
        .reshape(1, capacity, 1, 1)
    )
    columns = start_amplitudes.shape[3]
    block_points = radial_terms.shape[1]
    states = columns // (2 * block_points)
    points = potential.shape[0]
    blocks_all = points // block_points
    per_device = capacity // lax.axis_size("rad")
    first_row = lax.axis_index("rad") * per_device
    local_energy = lax.dynamic_slice_in_dim(energy[0], first_row, per_device)
    angles = local_energy[:, None] + potential[None, :]
    cosine = jnp.cos(angles)[None, :, None, :]
    sine = jnp.sin(angles)[None, :, None, :]
    radial_rows = jnp.broadcast_to(
        radial_terms[:, None, None, :], (orders, states, 2, block_points)
    ).reshape(orders, 1, columns)
    out_index = jnp.arange(columns, dtype=jnp.int32)
    out_part = out_index // block_points % 2
    in_index = out_index[:, None]
    swap_sign = jnp.where(
        (in_index == out_index[None, :] + block_points) & (out_part[None, :] == 0), 1.0, 0.0
    )
    swap_sign = swap_sign - jnp.where(
        (in_index == out_index[None, :] - block_points) & (out_part[None, :] == 1), 1.0, 0.0
    )
    swap_sign = swap_sign.astype(jnp.float32)

    def coupled_term(current):
        sent = current.astype(jnp.bfloat16)
        widened = extended(sent, (("sym", 0),), 1)
        product = jnp.dot(
            weights, widened.reshape(3 * capacity, columns), preferred_element_type=jnp.float32
        )
        product = product.reshape(orders, capacity, columns)
        coupled = jnp.sum(product * radial_rows, axis=0)
        return coupled.reshape(1, capacity, 1, columns) * live_rows

    def relay_block(amplitudes, repeats):
        channel_block = lax.all_to_all(amplitudes, "rad", split_axis=1, concat_axis=2, tiled=True)
        items = channel_block.shape[0]
        spread = channel_block.reshape(items, per_device, blocks_all, states, 2, block_points)
        spread = spread.transpose(0, 1, 3, 4, 2, 5).reshape(items, per_device, states, 2, points)
        for _ in range(repeats):
            spread = radial_half(spread, cosine, sine, element_matrices)
        folded = spread.reshape(items, per_device, states, 2, blocks_all, block_points)
        moved = folded.transpose(0, 1, 4, 2, 3, 5).reshape(items, per_device, blocks_all, columns)
        return lax.all_to_all(moved, "rad", split_axis=2, concat_axis=1, tiled=True)

    amplitudes = start_amplitudes * live_rows
    amplitudes = relay_block(amplitudes, 1)
    for step_index in range(TIME_STEPS):
        first = step_length * coupled_term(amplitudes)
        second = step_length / 2.0 * coupled_term(first)
        third = step_length / 3.0 * coupled_term(second)
        even_sum = amplitudes - second
        odd_sum = (first - third).reshape(capacity, columns)
        turned = jnp.dot(
            odd_sum, swap_sign, precision=lax.Precision.HIGHEST, preferred_element_type=jnp.float32
        )
        amplitudes = even_sum + turned.reshape(1, capacity, 1, columns)
        amplitudes = relay_block(amplitudes, 1 if step_index + 1 == TIME_STEPS else 2)
    return amplitudes


f32 = jnp.float32
bf16 = jnp.bfloat16
f16 = jnp.float16


def halves(x):
    high = x.astype(bf16)
    return high, (x - high.astype(f32)).astype(bf16)


def wide_halves(x):
    high, low = halves(x)
    return jnp.concatenate([high, low, high], axis=1)


def stacked_halves(x):
    high, low = halves(x)
    return jnp.concatenate([high, high, low], axis=0)


def split_three(x):
    parts = []
    for _ in range(2):
        scaled = x * 8193.0
        high = scaled - (scaled - x)
        parts.append(high)
        x = (x - high) * 2048.0
    return parts + [x]


def pack_kernel(count_ref, start_hbm, radial_hbm, out_ref, turn, start_ref, radial_ref, sems):
    capacity, columns = start_ref.shape
    copies = [
        pltpu.make_async_copy(start_hbm, start_ref, sems.at[0]),
        pltpu.make_async_copy(radial_hbm, radial_ref, sems.at[1]),
    ]
    for copy in copies:
        copy.start()
    hosts, rows, _ = out_ref.shape
    orders, block = radial_ref.shape
    states = columns // rows
    turn[...] = jnp.zeros_like(turn)
    for copy in copies:
        copy.wait()
    row = lax.broadcasted_iota(jnp.int32, (capacity, columns), 0)
    turned = jnp.where(row < count_ref[0], start_ref[...], 0.0).T
    for index, part in enumerate(split_three(radial_ref[...])):
        turn[8 * index : 8 * index + orders, :block] = part
    radial = turn[...].T[:block]
    for host in range(hosts):
        state = host // (hosts // states)
        out_ref[host, :, :capacity] = turned[state * rows : (state + 1) * rows]
        for p in range(2):
            out_ref[host, p * block : (p + 1) * block, capacity:] = radial


def unpack_kernel(place_ref, own_ref, *refs):
    pieces, out_ref, rows = refs[:-2], refs[-2], refs[-1]
    height = own_ref.shape[1]
    mine = place_ref[0]
    for turn, ref in enumerate([own_ref.at[mine]] + list(pieces)):
        state = jnp.bitwise_xor(mine, turn)
        rows[pl.ds(pl.multiple_of(state * height, height), height)] = ref[...].astype(f32)
    out_ref[...] = rows[...].T


def tables_kernel(angle_ref, radii_ref, matrix_ref, one_ref, two_ref, phase_ref, rows):
    m0 = matrix_ref[0]
    m1 = matrix_ref[1]
    cosine = jnp.cos(radii_ref[...])
    sine = jnp.sin(radii_ref[...])
    k0 = m0 * cosine + m1 * sine
    k1 = m1 * cosine - m0 * sine

    def store_pair(ref, real, imag):
        real, imag = real.T, imag.T
        upper = jnp.concatenate([real, imag], axis=1)
        lower = jnp.concatenate([-imag, real], axis=1)
        ref[...] = stacked_halves(jnp.concatenate([upper, lower], axis=0))

    def mm(x, y):
        return jnp.dot(x, y, precision=lax.Precision.HIGHEST, preferred_element_type=f32)

    store_pair(one_ref, k0, k1)
    store_pair(two_ref, mm(k0, k0) - mm(k1, k1), mm(k0, k1) + mm(k1, k0))
    angle = angle_ref[...]
    rows[...] = jnp.zeros_like(rows)
    for index, value in enumerate((jnp.cos(angle), jnp.sin(angle), jnp.cos(2.0 * angle), jnp.sin(2.0 * angle))):
        rows[2 * index : 2 * index + 2] = value
    phase_ref[...] = rows[...].T


def least_tiles(tiles):
    return (tiles + 1) // 2


def steps_kernel(
    orders,
    block,
    info_ref,
    own_w,
    other_w,
    own_x,
    other_x,
    one_half,
    two_half,
    phases,
    out_ref,
    weights,
    current,
    following,
    total,
    factors,
    selected,
    sems,
):
    tiles = weights.shape[1]
    tile = weights.shape[3]
    capacity = tiles * tile
    width = current.shape[1] // 2
    part, own, live = (info_ref[n] for n in range(3))
    head = 7

    def code(a, i, b, j):
        return info_ref[head + ((a * tiles + i) * 2 + b) * tiles + j]

    def fetch(source, a, i, b):
        return pltpu.make_async_copy(
            source.at[:, 1 if a == b else info_ref[5 + a], pl.ds(i * tile, tile)],
            weights.at[a, i, :, :, b * capacity : (b + 1) * capacity],
            sems.at[a, i, b],
        )

    def rows_of(a):
        return live if a else tiles

    def start_copies(source, a):
        def row(i, carry):
            for b in range(2):
                fetch(source, a, i, b).start()
            return carry

        lax.fori_loop(0, rows_of(a), row, 0)

    def settle(a):
        def row(i, carry):
            for b in range(2):
                fetch(own_w, a, i, b).wait()
                for j in range(tiles):
                    first = b * capacity + j * tile

                    @pl.when(code(a, i, b, j) == 0)
                    def _():
                        weights[a, i, :, :, first : first + tile] = jnp.zeros(
                            (orders, tile, tile), bf16
                        )

            return carry

        lax.fori_loop(0, rows_of(a), row, 0)

    for a in range(2):
        pl.when(own == a)(functools.partial(start_copies, own_w, a))
        pl.when(own != a)(functools.partial(start_copies, other_w, a))

    def rotated(v, a, first, col):
        rows = slice(first, first + v.shape[0])
        c = phases[rows, 4 * col + a : 4 * col + a + 1]
        s = phases[rows, 4 * col + 2 + a : 4 * col + 3 + a]
        real, imag = v[:, :width], v[:, width:]
        return jnp.concatenate([real * c + imag * s, imag * c - real * s], axis=1)

    def begin(a, first, v):
        total[a * capacity + first : a * capacity + first + v.shape[0]] = v
        current[a * capacity + first : a * capacity + first + v.shape[0]] = v.astype(bf16)

    for a in range(2):
        x = jnp.where(own == a, own_x[...], other_x[...])
        blocks = x.shape[0] // (2 * block)
        pieces = [
            x[(2 * n + p) * block : (2 * n + p + 1) * block]
            for p in range(2)
            for n in range(blocks)
        ]
        turned = jnp.concatenate(pieces, axis=0).T
        v = jnp.dot(wide_halves(turned[:capacity]), one_half[...], preferred_element_type=f32)
        begin(a, 0, rotated(v, a, 0, 0))
        settle(a)
        if a == 0:
            for l in range(orders):
                high, middle, low = (
                    turned[capacity + 8 * n + l : capacity + 8 * n + l + 1] for n in range(3)
                )
                factors[l : l + 1] = high + (middle + low / 2048.0) / 2048.0

    def couple(factor, second):
        radial = [factors[l : l + 1] * factor for l in range(orders)]
        depth = capacity + second * tile
        for a in range(2):
            count = info_ref[3 + a]
            for i in range(second if a else tiles):
                w = weights[a, i, :, :, :depth].reshape(orders * tile, depth)
                product = jnp.dot(w, current[:depth], preferred_element_type=f32)
                u = product[:tile] * radial[0]
                for l in range(1, orders):
                    u = u + product[l * tile : (l + 1) * tile] * radial[l]
                row = lax.broadcasted_iota(jnp.int32, u.shape, 0) + i * tile
                u = jnp.where(row < count, u, 0.0)
                term = jnp.concatenate([u[:, width:], -u[:, :width]], axis=1)
                first = a * capacity + i * tile
                total[first : first + tile] += term
                following[first : first + tile] = term.astype(bf16)
        current[:depth] = following[:depth]

    def run(index, carry):
        k = lax.rem(index, 3)

        @pl.when(jnp.logical_and(k == 0, index > 0))
        def _():
            high, low = halves(total[...])
            current[...] = high
            following[...] = low
            for a in range(2):
                rows = slice(a * capacity, (a + 1) * capacity)
                high = current[rows]
                v = jnp.dot(
                    jnp.concatenate([high, following[rows], high], axis=1),
                    two_half[...],
                    preferred_element_type=f32,
                )
                begin(a, 0, rotated(v, a, 0, 1))

        factor = jnp.where(k == 1, step_length / 2.0, step_length / 3.0)
        factor = jnp.where(k == 0, step_length, factor)
        for second in range(least_tiles(tiles), tiles + 1):
            pl.when(live == second)(functools.partial(couple, factor, second))
        return carry

    lax.fori_loop(0, 3 * TIME_STEPS, run, 0)

    pieces = out_ref.shape[0]
    spread = width // (block * pieces)
    v = total[pl.ds(pl.multiple_of(own * capacity, capacity), capacity)]
    v = wide_halves(jnp.where(own == 0, rotated(v, 0, 0, 0), rotated(v, 1, 0, 0)))
    selected[...] = jnp.dot(v, one_half[...], preferred_element_type=f32).T
    for m in range(pieces):
        for p in range(2):
            first = pl.multiple_of(p * width + (m * spread + part) * block, block)
            out_ref[m, p * block : (p + 1) * block] = selected[pl.ds(first, block)].astype(bf16)


def pair_shards(
    start_amplitudes,
    coupling,
    block_pattern,
    counts,
    radial_terms,
    energy,
    potential,
    element_matrices,
):
    orders, capacity = coupling.shape[1:3]
    tiles = block_pattern.shape[1]
    tile = capacity // tiles
    columns = start_amplitudes.shape[3]
    block = radial_terms.shape[1]
    width = element_matrices.shape[2]
    elements = element_matrices.shape[1]
    states = columns // (2 * block)
    group = width // block
    spread = group // states
    rows = 2 * block
    vmem = pl.BlockSpec(memory_space=pltpu.VMEM)
    smem = pl.BlockSpec(memory_space=pltpu.SMEM)
    hbm = pl.BlockSpec(memory_space=pltpu.HBM)
    swap = [(0, 1), (1, 0)]
    place = lax.axis_index("rad")
    me = lax.axis_index("sym")
    element = place // group

    lanes = 128
    other_energy = lax.ppermute(energy, "sym", swap)
    other_counts = lax.ppermute(counts, "sym", swap)
    other_pattern = lax.ppermute(block_pattern, "sym", swap)
    other_coupling = lax.ppermute(coupling, "sym", swap)
    radii = lax.dynamic_slice_in_dim(potential, element * width, width)
    matrices = lax.dynamic_index_in_dim(element_matrices, element, 1, keepdims=False)
    own = jnp.where(counts[0] == capacity, 0, 1)

    def by_slot(mine, others):
        return jnp.where(own == 0, jnp.stack([mine, others]), jnp.stack([others, mine]))

    aways = by_slot(2 - 2 * me, 2 * me)
    slot_counts = by_slot(counts[0], other_counts[0])
    present = by_slot(block_pattern[0], other_pattern[0])
    live = jnp.clip(-(-slot_counts[1] // tile), least_tiles(tiles), tiles)
    index = jnp.arange(tiles)
    side = present[:, :, 1]
    across = jnp.where((aways == 0)[:, None, None], present[:, :, 0], present[:, :, 2])
    slots = jnp.arange(2)
    table = jnp.where(
        (slots[:, None] == slots)[:, None, :, None], side[:, :, None], across[:, :, None]
    )
    idle = (slots[:, None] == 1) & (index >= live)
    table = jnp.where(idle[:, :, None, None] | idle[None, None], 2, table)
    info = jnp.concatenate(
        [
            jnp.stack([place % spread, own, live]),
            slot_counts,
            aways,
            table.reshape(-1),
        ]
    ).astype(jnp.int32)
    square = jax.ShapeDtypeStruct((6 * width, 2 * width), bf16)
    one_half, two_half, phases = pl.pallas_call(
        tables_kernel,
        out_shape=(square, square, jax.ShapeDtypeStruct((capacity, lanes), f32)),
        in_specs=[vmem] * 3,
        out_specs=(vmem,) * 3,
        scratch_shapes=[pltpu.VMEM((lanes, capacity), f32)],
        compiler_params=pltpu.CompilerParams(vmem_limit_bytes=6 << 20),
        name="tables",
    )(by_slot(energy[0], other_energy[0]), radii[None], matrices)

    packed = pl.pallas_call(
        pack_kernel,
        out_shape=jax.ShapeDtypeStruct((group, rows, capacity + lanes), f32),
        in_specs=[smem, hbm, hbm],
        out_specs=vmem,
        scratch_shapes=[
            pltpu.VMEM((lanes, lanes), f32),
            pltpu.VMEM((capacity, columns), f32),
            pltpu.VMEM((orders, block), f32),
            pltpu.SemaphoreType.DMA((2,)),
        ],
        compiler_params=pltpu.CompilerParams(vmem_limit_bytes=4 << 20),
        name="pack",
    )(
        counts,
        pltpu.with_memory_space_constraint(start_amplitudes.reshape(capacity, columns), pltpu.HBM),
        pltpu.with_memory_space_constraint(radial_terms, pltpu.HBM),
    )
    wide = [[e * group + d for d in range(group)] for e in range(elements)]
    gathered = lax.all_to_all(
        packed.astype(f16), "rad", split_axis=0, concat_axis=0, tiled=True, axis_index_groups=wide
    ).reshape(group * rows, capacity + lanes)
    other_gathered = lax.ppermute(gathered, "sym", swap)

    def by_order(x):
        return pltpu.with_memory_space_constraint(x[0].transpose(0, 2, 1, 3), pltpu.HBM)

    def body(*refs):
        steps_kernel(orders, block, *refs)

    result = pl.pallas_call(
        body,
        out_shape=jax.ShapeDtypeStruct((states, rows, capacity), bf16),
        in_specs=[smem, hbm, hbm] + [vmem] * 5,
        out_specs=vmem,
        scratch_shapes=[
            pltpu.VMEM((2, tiles, orders, tile, 2 * capacity), bf16),
            pltpu.VMEM((2 * capacity, 2 * width), bf16),
            pltpu.VMEM((2 * capacity, 2 * width), bf16),
            pltpu.VMEM((2 * capacity, 2 * width), f32),
            pltpu.VMEM((8, 2 * width), f32),
            pltpu.VMEM((2 * width, capacity), f32),
            pltpu.SemaphoreType.DMA((2, tiles, 2)),
        ],
        compiler_params=pltpu.CompilerParams(vmem_limit_bytes=28 << 20),
        name="steps",
    )(
        info,
        by_order(coupling),
        by_order(other_coupling),
        gathered.astype(f32),
        other_gathered.astype(f32),
        one_half,
        two_half,
        phases,
    )
    mine = (place % group) // spread
    received = []
    for turn in range(states - 1, 0, -1):
        pairs = [
            (e * group + n * spread + d, e * group + (n ^ turn) * spread + d)
            for e in range(elements)
            for n in range(states)
            for d in range(spread)
        ]
        piece = lax.dynamic_index_in_dim(result, mine ^ turn, 0, keepdims=False)
        received.insert(0, lax.ppermute(piece, "rad", pairs))
    out = pl.pallas_call(
        unpack_kernel,
        out_shape=jax.ShapeDtypeStruct((capacity, columns), f32),
        in_specs=[smem] + [vmem] * states,
        out_specs=vmem,
        scratch_shapes=[pltpu.VMEM((columns, capacity), f32)],
        compiler_params=pltpu.CompilerParams(vmem_limit_bytes=4 << 20),
        name="unpack",
    )(mine.astype(jnp.int32)[None], result, *received)
    return out.reshape(start_amplitudes.shape)


def solution(mesh):
    paired = mesh.shape["sym"] == 2

    def program(*args):
        states = args[0].shape[3] // (2 * args[4].shape[1])
        group = args[7].shape[2] // args[4].shape[1]
        if paired and group % states == 0 and states & (states - 1) == 0:
            return pair_shards(*args)
        return halo_shards(*args)

    return jax.shard_map(
        program,
        mesh=mesh,
        in_specs=(
            P("sym", None, "rad", None),
            P("sym", None, None, None, None),
            P("sym", None, None, None),
            P("sym"),
            P(None, "rad"),
            P("sym", None),
            P(),
            P(),
        ),
        out_specs=P("sym", None, "rad", None),
        check_vma=False,
    )
```

```python
import functools

import jax
import jax.numpy as jnp
from jax import lax
from jax.experimental import pallas as pl
from jax.experimental.pallas import tpu as pltpu
from jax.sharding import PartitionSpec as P

TIME_STEPS = 2


step_length = 0.8


def extended(x, sides, width):
    for axis, dim in sides:
        size, length = (lax.axis_size(axis), x.shape[dim])
        up = [(i, (i + 1) % size) for i in range(size - 1)]
        down = [(j, i) for i, j in up]
        last = lax.slice_in_dim(x, length - width, length, axis=dim)
        initial = lax.slice_in_dim(x, 0, width, axis=dim)
        before = lax.ppermute(last, axis, up)
        after = lax.ppermute(initial, axis, down)
        x = jnp.concatenate([before, x, after], axis=dim)
    return x


def element_product(real_part, imag_part, matrices):
    shape_in = real_part.shape
    elements = matrices.shape[1]
    width = matrices.shape[2]
    real_blocks = real_part.reshape(shape_in[:-1] + (elements, width))
    imag_blocks = imag_part.reshape(shape_in[:-1] + (elements, width))
    highest = lax.Precision.HIGHEST
    out_real = jnp.einsum(
        "abnej,eij->abnei", real_blocks, matrices[0], precision=highest
    ) - jnp.einsum("abnej,eij->abnei", imag_blocks, matrices[1], precision=highest)
    out_imag = jnp.einsum(
        "abnej,eij->abnei", imag_blocks, matrices[0], precision=highest
    ) + jnp.einsum("abnej,eij->abnei", real_blocks, matrices[1], precision=highest)
    return (out_real.reshape(shape_in), out_imag.reshape(shape_in))


def radial_half(channel_block, cosine, sine, matrices):
    real_part = channel_block[:, :, :, 0, :]
    imag_part = channel_block[:, :, :, 1, :]
    turned_real = real_part * cosine + imag_part * sine
    turned_imag = imag_part * cosine - real_part * sine
    out_real, out_imag = element_product(turned_real, turned_imag, matrices)
    return jnp.stack((out_real, out_imag), axis=3)


def halo_shards(
    start_amplitudes,
    coupling,
    block_pattern,
    counts,
    radial_terms,
    energy,
    potential,
    element_matrices,
):
    capacity = coupling.shape[2]
    orders = coupling.shape[1]
    tile_size = capacity // block_pattern.shape[1]
    pattern = jnp.repeat(jnp.repeat(block_pattern[0], tile_size, axis=0), tile_size, axis=2).astype(
        jnp.bfloat16
    )
    weights = (coupling[0] * pattern[None]).reshape(orders * capacity, 3 * capacity)
    live_rows = (
        (jnp.arange(capacity, dtype=jnp.int32) < counts[0])
        .astype(jnp.float32)
        .reshape(1, capacity, 1, 1)
    )
    columns = start_amplitudes.shape[3]
    block_points = radial_terms.shape[1]
    states = columns // (2 * block_points)
    points = potential.shape[0]
    blocks_all = points // block_points
    per_device = capacity // lax.axis_size("rad")
    first_row = lax.axis_index("rad") * per_device
    local_energy = lax.dynamic_slice_in_dim(energy[0], first_row, per_device)
    angles = local_energy[:, None] + potential[None, :]
    cosine = jnp.cos(angles)[None, :, None, :]
    sine = jnp.sin(angles)[None, :, None, :]
    radial_rows = jnp.broadcast_to(
        radial_terms[:, None, None, :], (orders, states, 2, block_points)
    ).reshape(orders, 1, columns)
    out_index = jnp.arange(columns, dtype=jnp.int32)
    out_part = out_index // block_points % 2
    in_index = out_index[:, None]
    swap_sign = jnp.where(
        (in_index == out_index[None, :] + block_points) & (out_part[None, :] == 0), 1.0, 0.0
    )
    swap_sign = swap_sign - jnp.where(
        (in_index == out_index[None, :] - block_points) & (out_part[None, :] == 1), 1.0, 0.0
    )
    swap_sign = swap_sign.astype(jnp.float32)

    def coupled_term(current):
        sent = current.astype(jnp.bfloat16)
        widened = extended(sent, (("sym", 0),), 1)
        product = jnp.dot(
            weights, widened.reshape(3 * capacity, columns), preferred_element_type=jnp.float32
        )
        product = product.reshape(orders, capacity, columns)
        coupled = jnp.sum(product * radial_rows, axis=0)
        return coupled.reshape(1, capacity, 1, columns) * live_rows

    def relay_block(amplitudes, repeats):
        channel_block = lax.all_to_all(amplitudes, "rad", split_axis=1, concat_axis=2, tiled=True)
        items = channel_block.shape[0]
        spread = channel_block.reshape(items, per_device, blocks_all, states, 2, block_points)
        spread = spread.transpose(0, 1, 3, 4, 2, 5).reshape(items, per_device, states, 2, points)
        for _ in range(repeats):
            spread = radial_half(spread, cosine, sine, element_matrices)
        folded = spread.reshape(items, per_device, states, 2, blocks_all, block_points)
        moved = folded.transpose(0, 1, 4, 2, 3, 5).reshape(items, per_device, blocks_all, columns)
        return lax.all_to_all(moved, "rad", split_axis=2, concat_axis=1, tiled=True)

    amplitudes = start_amplitudes * live_rows
    amplitudes = relay_block(amplitudes, 1)
    for step_index in range(TIME_STEPS):
        first = step_length * coupled_term(amplitudes)
        second = step_length / 2.0 * coupled_term(first)
        third = step_length / 3.0 * coupled_term(second)
        even_sum = amplitudes - second
        odd_sum = (first - third).reshape(capacity, columns)
        turned = jnp.dot(
            odd_sum, swap_sign, precision=lax.Precision.HIGHEST, preferred_element_type=jnp.float32
        )
        amplitudes = even_sum + turned.reshape(1, capacity, 1, columns)
        amplitudes = relay_block(amplitudes, 1 if step_index + 1 == TIME_STEPS else 2)
    return amplitudes


f32 = jnp.float32
bf16 = jnp.bfloat16
f16 = jnp.float16


def halves(x):
    high = x.astype(bf16)
    return high, (x - high.astype(f32)).astype(bf16)


def wide_halves(x):
    high, low = halves(x)
    return jnp.concatenate([high, low, high], axis=1)


def stacked_halves(x):
    high, low = halves(x)
    return jnp.concatenate([high, high, low], axis=0)


def split_three(x):
    parts = []
    for _ in range(2):
        scaled = x * 8193.0
        high = scaled - (scaled - x)
        parts.append(high)
        x = (x - high) * 2048.0
    return parts + [x]


def pack_kernel(count_ref, start_hbm, radial_hbm, out_ref, turn, start_ref, radial_ref, sems):
    capacity, columns = start_ref.shape
    copies = [
        pltpu.make_async_copy(start_hbm, start_ref, sems.at[0]),
        pltpu.make_async_copy(radial_hbm, radial_ref, sems.at[1]),
    ]
    for copy in copies:
        copy.start()
    hosts, rows, _ = out_ref.shape
    orders, block = radial_ref.shape
    states = columns // rows
    turn[...] = jnp.zeros_like(turn)
    for copy in copies:
        copy.wait()
    row = lax.broadcasted_iota(jnp.int32, (capacity, columns), 0)
    turned = jnp.where(row < count_ref[0], start_ref[...], 0.0).T
    for index, part in enumerate(split_three(radial_ref[...])):
        turn[8 * index : 8 * index + orders, :block] = part
    radial = turn[...].T[:block]
    for host in range(hosts):
        state = host // (hosts // states)
        out_ref[host, :, :capacity] = turned[state * rows : (state + 1) * rows]
        for p in range(2):
            out_ref[host, p * block : (p + 1) * block, capacity:] = radial


def unpack_kernel(place_ref, own_ref, *refs):
    pieces, out_ref, rows = refs[:-2], refs[-2], refs[-1]
    height = own_ref.shape[1]
    mine = place_ref[0]
    for turn, ref in enumerate([own_ref.at[mine]] + list(pieces)):
        state = jnp.bitwise_xor(mine, turn)
        rows[pl.ds(pl.multiple_of(state * height, height), height)] = ref[...].astype(f32)
    out_ref[...] = rows[...].T


def tables_kernel(angle_ref, radii_ref, matrix_ref, one_ref, two_ref, phase_ref, rows):
    m0 = matrix_ref[0]
    m1 = matrix_ref[1]
    cosine = jnp.cos(radii_ref[...])
    sine = jnp.sin(radii_ref[...])
    k0 = m0 * cosine + m1 * sine
    k1 = m1 * cosine - m0 * sine

    def store_pair(ref, real, imag):
        real, imag = real.T, imag.T
        upper = jnp.concatenate([real, imag], axis=1)
        lower = jnp.concatenate([-imag, real], axis=1)
        ref[...] = stacked_halves(jnp.concatenate([upper, lower], axis=0))

    def mm(x, y):
        return jnp.dot(x, y, precision=lax.Precision.HIGHEST, preferred_element_type=f32)

    store_pair(one_ref, k0, k1)
    store_pair(two_ref, mm(k0, k0) - mm(k1, k1), mm(k0, k1) + mm(k1, k0))
    angle = angle_ref[...]
    rows[...] = jnp.zeros_like(rows)
    for index, value in enumerate((jnp.cos(angle), jnp.sin(angle), jnp.cos(2.0 * angle), jnp.sin(2.0 * angle))):
        rows[2 * index : 2 * index + 2] = value
    phase_ref[...] = rows[...].T


def least_tiles(tiles):
    return (tiles + 1) // 2


def steps_kernel(
    orders,
    block,
    info_ref,
    own_w,
    other_w,
    own_x,
    other_x,
    one_half,
    two_half,
    phases,
    masks,
    out_ref,
    weights,
    current,
    following,
    total,
    factors,
    selected,
    sems,
):
    tiles = weights.shape[1]
    tile = weights.shape[3]
    capacity = tiles * tile
    width = current.shape[1] // 2
    part, own, live = (info_ref[n] for n in range(3))

    def fetch(source, a, i, b):
        return pltpu.make_async_copy(
            source.at[:, 1 if a == b else info_ref[5 + a], pl.ds(i * tile, tile)],
            weights.at[a, i, :, :, b * capacity : (b + 1) * capacity],
            sems.at[a, i, b],
        )

    def rows_of(a):
        return live if a else tiles

    def start_copies(source, a):
        def row(i, carry):
            for b in range(2):
                fetch(source, a, i, b).start()
            return carry

        lax.fori_loop(0, rows_of(a), row, 0)

    for a in range(2):
        pl.when(own == a)(functools.partial(start_copies, own_w, a))
        pl.when(own != a)(functools.partial(start_copies, other_w, a))

    def rotated(v, a, first, col):
        rows = slice(first, first + v.shape[0])
        c = phases[rows, 4 * col + a : 4 * col + a + 1]
        s = phases[rows, 4 * col + 2 + a : 4 * col + 3 + a]
        real, imag = v[:, :width], v[:, width:]
        return jnp.concatenate([real * c + imag * s, imag * c - real * s], axis=1)

    def begin(a, first, v):
        total[a * capacity + first : a * capacity + first + v.shape[0]] = v
        current[a * capacity + first : a * capacity + first + v.shape[0]] = v.astype(bf16)

    for a in range(2):
        x = jnp.where(own == a, own_x[...], other_x[...])
        blocks = x.shape[0] // (2 * block)
        pieces = [
            x[(2 * n + p) * block : (2 * n + p + 1) * block]
            for p in range(2)
            for n in range(blocks)
        ]
        turned = jnp.concatenate(pieces, axis=0).T
        v = jnp.dot(wide_halves(turned[:capacity]), one_half[...], preferred_element_type=f32)
        begin(a, 0, rotated(v, a, 0, 0))
        if a == 0:
            for l in range(orders):
                high, middle, low = (
                    turned[capacity + 8 * n + l : capacity + 8 * n + l + 1] for n in range(3)
                )
                factors[l : l + 1] = high + (middle + low / 2048.0) / 2048.0

    def couple(factor, second, first_pass=False):
        radial = [factors[l : l + 1] * factor for l in range(orders)]
        depth = capacity + second * tile
        for a in range(2):
            count = info_ref[3 + a]
            if first_pass:
                for i in range(second if a else tiles):
                    for b in range(2):
                        fetch(own_w, a, i, b).wait()
            for i in range(second if a else tiles):
                if first_pass:
                    w = weights[a, i, :, :, :depth] * masks[a, i : i + 1, :depth]
                    weights[a, i, :, :, :depth] = w
                    w = w.reshape(orders * tile, depth)
                else:
                    w = weights[a, i, :, :, :depth].reshape(orders * tile, depth)
                product = jnp.dot(w, current[:depth], preferred_element_type=f32)
                u = product[:tile] * radial[0]
                for l in range(1, orders):
                    u = u + product[l * tile : (l + 1) * tile] * radial[l]
                row = lax.broadcasted_iota(jnp.int32, u.shape, 0) + i * tile
                u = jnp.where(row < count, u, 0.0)
                term = jnp.concatenate([u[:, width:], -u[:, :width]], axis=1)
                first = a * capacity + i * tile
                total[first : first + tile] += term
                following[first : first + tile] = term.astype(bf16)
        current[:depth] = following[:depth]

    def run(index, carry):
        k = lax.rem(index, 3)

        @pl.when(k == 0)
        def _():
            high, low = halves(total[...])
            current[...] = high
            following[...] = low
            for a in range(2):
                rows = slice(a * capacity, (a + 1) * capacity)
                high = current[rows]
                v = jnp.dot(
                    jnp.concatenate([high, following[rows], high], axis=1),
                    two_half[...],
                    preferred_element_type=f32,
                )
                begin(a, 0, rotated(v, a, 0, 1))

        factor = jnp.where(k == 1, step_length / 2.0, step_length / 3.0)
        factor = jnp.where(k == 0, step_length, factor)
        for second in range(least_tiles(tiles), tiles + 1):
            pl.when(live == second)(functools.partial(couple, factor, second))
        return carry

    for second in range(least_tiles(tiles), tiles + 1):
        pl.when(live == second)(functools.partial(couple, step_length, second, True))
    lax.fori_loop(1, 3 * TIME_STEPS, run, 0)

    pieces = out_ref.shape[0]
    spread = width // (block * pieces)
    v = total[pl.ds(pl.multiple_of(own * capacity, capacity), capacity)]
    v = wide_halves(jnp.where(own == 0, rotated(v, 0, 0, 0), rotated(v, 1, 0, 0)))
    selected[...] = jnp.dot(v, one_half[...], preferred_element_type=f32).T
    for m in range(pieces):
        for p in range(2):
            first = pl.multiple_of(p * width + (m * spread + part) * block, block)
            out_ref[m, p * block : (p + 1) * block] = selected[pl.ds(first, block)].astype(bf16)


def pair_shards(
    start_amplitudes,
    coupling,
    block_pattern,
    counts,
    radial_terms,
    energy,
    potential,
    element_matrices,
):
    orders, capacity = coupling.shape[1:3]
    tiles = block_pattern.shape[1]
    tile = capacity // tiles
    columns = start_amplitudes.shape[3]
    block = radial_terms.shape[1]
    width = element_matrices.shape[2]
    elements = element_matrices.shape[1]
    states = columns // (2 * block)
    group = width // block
    spread = group // states
    rows = 2 * block
    vmem = pl.BlockSpec(memory_space=pltpu.VMEM)
    smem = pl.BlockSpec(memory_space=pltpu.SMEM)
    hbm = pl.BlockSpec(memory_space=pltpu.HBM)
    swap = [(0, 1), (1, 0)]
    place = lax.axis_index("rad")
    me = lax.axis_index("sym")
    element = place // group

    lanes = 128
    other_energy = lax.ppermute(energy, "sym", swap)
    other_counts = lax.ppermute(counts, "sym", swap)
    other_pattern = lax.ppermute(block_pattern, "sym", swap)
    other_coupling = lax.ppermute(coupling, "sym", swap)
    radii = lax.dynamic_slice_in_dim(potential, element * width, width)
    matrices = lax.dynamic_index_in_dim(element_matrices, element, 1, keepdims=False)
    own = jnp.where(counts[0] == capacity, 0, 1)

    def by_slot(mine, others):
        return jnp.where(own == 0, jnp.stack([mine, others]), jnp.stack([others, mine]))

    aways = by_slot(2 - 2 * me, 2 * me)
    slot_counts = by_slot(counts[0], other_counts[0])
    present = by_slot(block_pattern[0], other_pattern[0])
    live = jnp.clip(-(-slot_counts[1] // tile), least_tiles(tiles), tiles)
    side = present[:, :, 1]
    across = jnp.where((aways == 0)[:, None, None], present[:, :, 0], present[:, :, 2])
    slots = jnp.arange(2)
    table = jnp.where(
        (slots[:, None] == slots)[:, None, :, None], side[:, :, None], across[:, :, None]
    )
    masks = jnp.repeat(table.reshape(2, tiles, 2 * tiles), tile, axis=2).astype(bf16)
    info = jnp.concatenate([jnp.stack([place % spread, own, live]), slot_counts, aways])
    info = info.astype(jnp.int32)
    square = jax.ShapeDtypeStruct((6 * width, 2 * width), bf16)
    one_half, two_half, phases = pl.pallas_call(
        tables_kernel,
        out_shape=(square, square, jax.ShapeDtypeStruct((capacity, lanes), f32)),
        in_specs=[vmem] * 3,
        out_specs=(vmem,) * 3,
        scratch_shapes=[pltpu.VMEM((lanes, capacity), f32)],
        compiler_params=pltpu.CompilerParams(vmem_limit_bytes=6 << 20),
        name="tables",
    )(by_slot(energy[0], other_energy[0]), radii[None], matrices)

    packed = pl.pallas_call(
        pack_kernel,
        out_shape=jax.ShapeDtypeStruct((group, rows, capacity + lanes), f32),
        in_specs=[smem, hbm, hbm],
        out_specs=vmem,
        scratch_shapes=[
            pltpu.VMEM((lanes, lanes), f32),
            pltpu.VMEM((capacity, columns), f32),
            pltpu.VMEM((orders, block), f32),
            pltpu.SemaphoreType.DMA((2,)),
        ],
        compiler_params=pltpu.CompilerParams(vmem_limit_bytes=4 << 20),
        name="pack",
    )(
        counts,
        pltpu.with_memory_space_constraint(start_amplitudes.reshape(capacity, columns), pltpu.HBM),
        pltpu.with_memory_space_constraint(radial_terms, pltpu.HBM),
    )
    wide = [[e * group + d for d in range(group)] for e in range(elements)]
    gathered = lax.all_to_all(
        packed.astype(f16), "rad", split_axis=0, concat_axis=0, tiled=True, axis_index_groups=wide
    ).reshape(group * rows, capacity + lanes)
    other_gathered = lax.ppermute(gathered, "sym", swap)

    def by_order(x):
        return pltpu.with_memory_space_constraint(x[0].transpose(0, 2, 1, 3), pltpu.HBM)

    def body(*refs):
        steps_kernel(orders, block, *refs)

    result = pl.pallas_call(
        body,
        out_shape=jax.ShapeDtypeStruct((states, rows, capacity), bf16),
        in_specs=[smem, hbm, hbm] + [vmem] * 6,
        out_specs=vmem,
        scratch_shapes=[
            pltpu.VMEM((2, tiles, orders, tile, 2 * capacity), bf16),
            pltpu.VMEM((2 * capacity, 2 * width), bf16),
            pltpu.VMEM((2 * capacity, 2 * width), bf16),
            pltpu.VMEM((2 * capacity, 2 * width), f32),
            pltpu.VMEM((8, 2 * width), f32),
            pltpu.VMEM((2 * width, capacity), f32),
            pltpu.SemaphoreType.DMA((2, tiles, 2)),
        ],
        compiler_params=pltpu.CompilerParams(vmem_limit_bytes=28 << 20),
        name="steps",
    )(
        info,
        by_order(coupling),
        by_order(other_coupling),
        gathered.astype(f32),
        other_gathered.astype(f32),
        one_half,
        two_half,
        phases,
        masks,
    )
    mine = (place % group) // spread
    received = []
    for turn in range(states - 1, 0, -1):
        pairs = [
            (e * group + n * spread + d, e * group + (n ^ turn) * spread + d)
            for e in range(elements)
            for n in range(states)
            for d in range(spread)
        ]
        piece = lax.dynamic_index_in_dim(result, mine ^ turn, 0, keepdims=False)
        received.insert(0, lax.ppermute(piece, "rad", pairs))
    out = pl.pallas_call(
        unpack_kernel,
        out_shape=jax.ShapeDtypeStruct((capacity, columns), f32),
        in_specs=[smem] + [vmem] * states,
        out_specs=vmem,
        scratch_shapes=[pltpu.VMEM((columns, capacity), f32)],
        compiler_params=pltpu.CompilerParams(vmem_limit_bytes=4 << 20),
        name="unpack",
    )(mine.astype(jnp.int32)[None], result, *received)
    return out.reshape(start_amplitudes.shape)


def solution(mesh):
    paired = mesh.shape["sym"] == 2

    def program(*args):
        states = args[0].shape[3] // (2 * args[4].shape[1])
        group = args[7].shape[2] // args[4].shape[1]
        if paired and group % states == 0 and states & (states - 1) == 0:
            return pair_shards(*args)
        return halo_shards(*args)

    return jax.shard_map(
        program,
        mesh=mesh,
        in_specs=(
            P("sym", None, "rad", None),
            P("sym", None, None, None, None),
            P("sym", None, None, None),
            P("sym"),
            P(None, "rad"),
            P("sym", None),
            P(),
            P(),
        ),
        out_specs=P("sym", None, "rad", None),
        check_vma=False,
    )
```

```python
import functools

import jax
import jax.numpy as jnp
from jax import lax
from jax.experimental import pallas as pl
from jax.experimental.pallas import tpu as pltpu
from jax.sharding import PartitionSpec as P

TIME_STEPS = 2


step_length = 0.8


def extended(x, sides, width):
    for axis, dim in sides:
        size, length = (lax.axis_size(axis), x.shape[dim])
        up = [(i, (i + 1) % size) for i in range(size - 1)]
        down = [(j, i) for i, j in up]
        last = lax.slice_in_dim(x, length - width, length, axis=dim)
        initial = lax.slice_in_dim(x, 0, width, axis=dim)
        before = lax.ppermute(last, axis, up)
        after = lax.ppermute(initial, axis, down)
        x = jnp.concatenate([before, x, after], axis=dim)
    return x


def element_product(real_part, imag_part, matrices):
    shape_in = real_part.shape
    elements = matrices.shape[1]
    width = matrices.shape[2]
    real_blocks = real_part.reshape(shape_in[:-1] + (elements, width))
    imag_blocks = imag_part.reshape(shape_in[:-1] + (elements, width))
    highest = lax.Precision.HIGHEST
    out_real = jnp.einsum(
        "abnej,eij->abnei", real_blocks, matrices[0], precision=highest
    ) - jnp.einsum("abnej,eij->abnei", imag_blocks, matrices[1], precision=highest)
    out_imag = jnp.einsum(
        "abnej,eij->abnei", imag_blocks, matrices[0], precision=highest
    ) + jnp.einsum("abnej,eij->abnei", real_blocks, matrices[1], precision=highest)
    return (out_real.reshape(shape_in), out_imag.reshape(shape_in))


def radial_half(channel_block, cosine, sine, matrices):
    real_part = channel_block[:, :, :, 0, :]
    imag_part = channel_block[:, :, :, 1, :]
    turned_real = real_part * cosine + imag_part * sine
    turned_imag = imag_part * cosine - real_part * sine
    out_real, out_imag = element_product(turned_real, turned_imag, matrices)
    return jnp.stack((out_real, out_imag), axis=3)


def halo_shards(
    start_amplitudes,
    coupling,
    block_pattern,
    counts,
    radial_terms,
    energy,
    potential,
    element_matrices,
):
    capacity = coupling.shape[2]
    orders = coupling.shape[1]
    tile_size = capacity // block_pattern.shape[1]
    pattern = jnp.repeat(jnp.repeat(block_pattern[0], tile_size, axis=0), tile_size, axis=2).astype(
        jnp.bfloat16
    )
    weights = (coupling[0] * pattern[None]).reshape(orders * capacity, 3 * capacity)
    live_rows = (
        (jnp.arange(capacity, dtype=jnp.int32) < counts[0])
        .astype(jnp.float32)
        .reshape(1, capacity, 1, 1)
    )
    columns = start_amplitudes.shape[3]
    block_points = radial_terms.shape[1]
    states = columns // (2 * block_points)
    points = potential.shape[0]
    blocks_all = points // block_points
    per_device = capacity // lax.axis_size("rad")
    first_row = lax.axis_index("rad") * per_device
    local_energy = lax.dynamic_slice_in_dim(energy[0], first_row, per_device)
    angles = local_energy[:, None] + potential[None, :]
    cosine = jnp.cos(angles)[None, :, None, :]
    sine = jnp.sin(angles)[None, :, None, :]
    radial_rows = jnp.broadcast_to(
        radial_terms[:, None, None, :], (orders, states, 2, block_points)
    ).reshape(orders, 1, columns)
    out_index = jnp.arange(columns, dtype=jnp.int32)
    out_part = out_index // block_points % 2
    in_index = out_index[:, None]
    swap_sign = jnp.where(
        (in_index == out_index[None, :] + block_points) & (out_part[None, :] == 0), 1.0, 0.0
    )
    swap_sign = swap_sign - jnp.where(
        (in_index == out_index[None, :] - block_points) & (out_part[None, :] == 1), 1.0, 0.0
    )
    swap_sign = swap_sign.astype(jnp.float32)

    def coupled_term(current):
        sent = current.astype(jnp.bfloat16)
        widened = extended(sent, (("sym", 0),), 1)
        product = jnp.dot(
            weights, widened.reshape(3 * capacity, columns), preferred_element_type=jnp.float32
        )
        product = product.reshape(orders, capacity, columns)
        coupled = jnp.sum(product * radial_rows, axis=0)
        return coupled.reshape(1, capacity, 1, columns) * live_rows

    def relay_block(amplitudes, repeats):
        channel_block = lax.all_to_all(amplitudes, "rad", split_axis=1, concat_axis=2, tiled=True)
        items = channel_block.shape[0]
        spread = channel_block.reshape(items, per_device, blocks_all, states, 2, block_points)
        spread = spread.transpose(0, 1, 3, 4, 2, 5).reshape(items, per_device, states, 2, points)
        for _ in range(repeats):
            spread = radial_half(spread, cosine, sine, element_matrices)
        folded = spread.reshape(items, per_device, states, 2, blocks_all, block_points)
        moved = folded.transpose(0, 1, 4, 2, 3, 5).reshape(items, per_device, blocks_all, columns)
        return lax.all_to_all(moved, "rad", split_axis=2, concat_axis=1, tiled=True)

    amplitudes = start_amplitudes * live_rows
    amplitudes = relay_block(amplitudes, 1)
    for step_index in range(TIME_STEPS):
        first = step_length * coupled_term(amplitudes)
        second = step_length / 2.0 * coupled_term(first)
        third = step_length / 3.0 * coupled_term(second)
        even_sum = amplitudes - second
        odd_sum = (first - third).reshape(capacity, columns)
        turned = jnp.dot(
            odd_sum, swap_sign, precision=lax.Precision.HIGHEST, preferred_element_type=jnp.float32
        )
        amplitudes = even_sum + turned.reshape(1, capacity, 1, columns)
        amplitudes = relay_block(amplitudes, 1 if step_index + 1 == TIME_STEPS else 2)
    return amplitudes


f32 = jnp.float32
bf16 = jnp.bfloat16
f16 = jnp.float16


def halves(x):
    high = x.astype(bf16)
    return high, (x - high.astype(f32)).astype(bf16)


def wide_halves(x):
    high, low = halves(x)
    return jnp.concatenate([high, low, high], axis=1)


def stacked_halves(x):
    high, low = halves(x)
    return jnp.concatenate([high, high, low], axis=0)


def split_three(x):
    parts = []
    for _ in range(2):
        scaled = x * 8193.0
        high = scaled - (scaled - x)
        parts.append(high)
        x = (x - high) * 2048.0
    return parts + [x]


def pack_kernel(count_ref, start_hbm, radial_hbm, out_ref, turn, start_ref, radial_ref, sems):
    capacity, columns = start_ref.shape
    copies = [
        pltpu.make_async_copy(start_hbm, start_ref, sems.at[0]),
        pltpu.make_async_copy(radial_hbm, radial_ref, sems.at[1]),
    ]
    for copy in copies:
        copy.start()
    hosts, rows, _ = out_ref.shape
    orders, block = radial_ref.shape
    states = columns // rows
    turn[...] = jnp.zeros_like(turn)
    for copy in copies:
        copy.wait()
    row = lax.broadcasted_iota(jnp.int32, (capacity, columns), 0)
    turned = jnp.where(row < count_ref[0], start_ref[...], 0.0).T
    for index, part in enumerate(split_three(radial_ref[...])):
        turn[8 * index : 8 * index + orders, :block] = part
    radial = turn[...].T[:block]
    for host in range(hosts):
        state = host // (hosts // states)
        out_ref[host, :, :capacity] = turned[state * rows : (state + 1) * rows]
        for p in range(2):
            out_ref[host, p * block : (p + 1) * block, capacity:] = radial


def unpack_kernel(place_ref, own_ref, *refs):
    pieces, (out_hbm, rows, turned, sems) = refs[:-4], refs[-4:]
    height = own_ref.shape[1]
    lanes = rows.shape[0]
    mine = place_ref[0]
    for turn, ref in enumerate([own_ref.at[mine]] + list(pieces)):
        state = jnp.bitwise_xor(mine, turn)
        rows[pl.ds(pl.multiple_of(state * height, height), height)] = ref[...].astype(f32)
    copies = []
    for n in range(sems.shape[0]):
        part = slice(n * lanes, (n + 1) * lanes)
        turned[part] = rows[:, part].T
        copies.append(pltpu.make_async_copy(turned.at[part], out_hbm.at[part], sems.at[n]))
        copies[-1].start()
    for copy in copies:
        copy.wait()


def tables_kernel(angle_ref, radii_ref, matrix_ref, one_ref, two_ref, phase_ref, rows):
    m0 = matrix_ref[0]
    m1 = matrix_ref[1]
    cosine = jnp.cos(radii_ref[...])
    sine = jnp.sin(radii_ref[...])
    k0 = m0 * cosine + m1 * sine
    k1 = m1 * cosine - m0 * sine

    def store_pair(ref, real, imag):
        real, imag = real.T, imag.T
        upper = jnp.concatenate([real, imag], axis=1)
        lower = jnp.concatenate([-imag, real], axis=1)
        ref[...] = stacked_halves(jnp.concatenate([upper, lower], axis=0))

    def mm(x, y):
        return jnp.dot(x, y, precision=lax.Precision.HIGHEST, preferred_element_type=f32)

    store_pair(one_ref, k0, k1)
    store_pair(two_ref, mm(k0, k0) - mm(k1, k1), mm(k0, k1) + mm(k1, k0))
    angle = angle_ref[...]
    rows[...] = jnp.zeros_like(rows)
    for index, value in enumerate((jnp.cos(angle), jnp.sin(angle), jnp.cos(2.0 * angle), jnp.sin(2.0 * angle))):
        rows[2 * index : 2 * index + 2] = value
    phase_ref[...] = rows[...].T


def least_tiles(tiles):
    return (tiles + 1) // 2


def steps_kernel(
    orders,
    block,
    info_ref,
    own_w,
    other_w,
    own_x,
    other_x,
    one_half,
    two_half,
    phases,
    masks,
    out_ref,
    weights,
    current,
    following,
    total,
    factors,
    selected,
    sems,
):
    tiles = weights.shape[1]
    tile = weights.shape[3]
    capacity = tiles * tile
    width = current.shape[1] // 2
    part, own, live = (info_ref[n] for n in range(3))

    def fetch(source, a, i, b):
        return pltpu.make_async_copy(
            source.at[:, 1 if a == b else info_ref[5 + a], pl.ds(i * tile, tile)],
            weights.at[a, i, :, :, b * capacity : (b + 1) * capacity],
            sems.at[a, i, b],
        )

    def rows_of(a):
        return live if a else tiles

    def start_copies(source, a):
        def row(i, carry):
            for b in range(2):
                fetch(source, a, i, b).start()
            return carry

        lax.fori_loop(0, rows_of(a), row, 0)

    for a in range(2):
        pl.when(own == a)(functools.partial(start_copies, own_w, a))
        pl.when(own != a)(functools.partial(start_copies, other_w, a))

    def rotated(v, a, first, col):
        rows = slice(first, first + v.shape[0])
        c = phases[rows, 4 * col + a : 4 * col + a + 1]
        s = phases[rows, 4 * col + 2 + a : 4 * col + 3 + a]
        real, imag = v[:, :width], v[:, width:]
        return jnp.concatenate([real * c + imag * s, imag * c - real * s], axis=1)

    def begin(a, first, v):
        total[a * capacity + first : a * capacity + first + v.shape[0]] = v
        current[a * capacity + first : a * capacity + first + v.shape[0]] = v.astype(bf16)

    for a in range(2):
        x = jnp.where(own == a, own_x[...], other_x[...])
        blocks = x.shape[0] // (2 * block)
        pieces = [
            x[(2 * n + p) * block : (2 * n + p + 1) * block]
            for p in range(2)
            for n in range(blocks)
        ]
        turned = jnp.concatenate(pieces, axis=0).T
        v = jnp.dot(wide_halves(turned[:capacity]), one_half[...], preferred_element_type=f32)
        begin(a, 0, rotated(v, a, 0, 0))
        if a == 0:
            for l in range(orders):
                high, middle, low = (
                    turned[capacity + 8 * n + l : capacity + 8 * n + l + 1] for n in range(3)
                )
                factors[l : l + 1] = high + (middle + low / 2048.0) / 2048.0

    def couple(factor, second, first_pass=False):
        radial = [factors[l : l + 1] * factor for l in range(orders)]
        depth = capacity + second * tile
        for a in range(2):
            count = info_ref[3 + a]
            if first_pass:
                for i in range(second if a else tiles):
                    for b in range(2):
                        fetch(own_w, a, i, b).wait()
            for i in range(second if a else tiles):
                if first_pass:
                    w = weights[a, i, :, :, :depth] * masks[a, i : i + 1, :depth]
                    weights[a, i, :, :, :depth] = w
                    w = w.reshape(orders * tile, depth)
                else:
                    w = weights[a, i, :, :, :depth].reshape(orders * tile, depth)
                product = jnp.dot(w, current[:depth], preferred_element_type=f32)
                u = product[:tile] * radial[0]
                for l in range(1, orders):
                    u = u + product[l * tile : (l + 1) * tile] * radial[l]
                row = lax.broadcasted_iota(jnp.int32, u.shape, 0) + i * tile
                u = jnp.where(row < count, u, 0.0)
                term = jnp.concatenate([u[:, width:], -u[:, :width]], axis=1)
                first = a * capacity + i * tile
                total[first : first + tile] += term
                following[first : first + tile] = term.astype(bf16)
        current[:depth] = following[:depth]

    def run(index, carry):
        k = lax.rem(index, 3)

        @pl.when(k == 0)
        def _():
            high, low = halves(total[...])
            current[...] = high
            following[...] = low
            for a in range(2):
                rows = slice(a * capacity, (a + 1) * capacity)
                high = current[rows]
                v = jnp.dot(
                    jnp.concatenate([high, following[rows], high], axis=1),
                    two_half[...],
                    preferred_element_type=f32,
                )
                begin(a, 0, rotated(v, a, 0, 1))

        factor = jnp.where(k == 1, step_length / 2.0, step_length / 3.0)
        factor = jnp.where(k == 0, step_length, factor)
        for second in range(least_tiles(tiles), tiles + 1):
            pl.when(live == second)(functools.partial(couple, factor, second))
        return carry

    for second in range(least_tiles(tiles), tiles + 1):
        pl.when(live == second)(functools.partial(couple, step_length, second, True))
    lax.fori_loop(1, 3 * TIME_STEPS, run, 0)

    pieces = out_ref.shape[0]
    spread = width // (block * pieces)
    v = total[pl.ds(pl.multiple_of(own * capacity, capacity), capacity)]
    v = wide_halves(jnp.where(own == 0, rotated(v, 0, 0, 0), rotated(v, 1, 0, 0)))
    selected[...] = jnp.dot(v, one_half[...], preferred_element_type=f32).T
    for m in range(pieces):
        for p in range(2):
            first = pl.multiple_of(p * width + (m * spread + part) * block, block)
            out_ref[m, p * block : (p + 1) * block] = selected[pl.ds(first, block)].astype(bf16)


def pair_shards(
    start_amplitudes,
    coupling,
    block_pattern,
    counts,
    radial_terms,
    energy,
    potential,
    element_matrices,
):
    orders, capacity = coupling.shape[1:3]
    tiles = block_pattern.shape[1]
    tile = capacity // tiles
    columns = start_amplitudes.shape[3]
    block = radial_terms.shape[1]
    width = element_matrices.shape[2]
    elements = element_matrices.shape[1]
    states = columns // (2 * block)
    group = width // block
    spread = group // states
    rows = 2 * block
    vmem = pl.BlockSpec(memory_space=pltpu.VMEM)
    smem = pl.BlockSpec(memory_space=pltpu.SMEM)
    hbm = pl.BlockSpec(memory_space=pltpu.HBM)
    swap = [(0, 1), (1, 0)]
    place = lax.axis_index("rad")
    me = lax.axis_index("sym")
    element = place // group

    lanes = 128
    other_energy = lax.ppermute(energy, "sym", swap)
    other_counts = lax.ppermute(counts, "sym", swap)
    other_pattern = lax.ppermute(block_pattern, "sym", swap)
    other_coupling = lax.ppermute(coupling, "sym", swap)
    radii = lax.dynamic_slice_in_dim(potential, element * width, width)
    matrices = lax.dynamic_index_in_dim(element_matrices, element, 1, keepdims=False)
    own = jnp.where(counts[0] == capacity, 0, 1)

    def by_slot(mine, others):
        return jnp.where(own == 0, jnp.stack([mine, others]), jnp.stack([others, mine]))

    aways = by_slot(2 - 2 * me, 2 * me)
    slot_counts = by_slot(counts[0], other_counts[0])
    present = by_slot(block_pattern[0], other_pattern[0])
    live = jnp.clip(-(-slot_counts[1] // tile), least_tiles(tiles), tiles)
    side = present[:, :, 1]
    across = jnp.where((aways == 0)[:, None, None], present[:, :, 0], present[:, :, 2])
    slots = jnp.arange(2)
    table = jnp.where(
        (slots[:, None] == slots)[:, None, :, None], side[:, :, None], across[:, :, None]
    )
    masks = jnp.repeat(table.reshape(2, tiles, 2 * tiles), tile, axis=2).astype(bf16)
    info = jnp.concatenate([jnp.stack([place % spread, own, live]), slot_counts, aways])
    info = info.astype(jnp.int32)
    square = jax.ShapeDtypeStruct((6 * width, 2 * width), bf16)
    one_half, two_half, phases = pl.pallas_call(
        tables_kernel,
        out_shape=(square, square, jax.ShapeDtypeStruct((capacity, lanes), f32)),
        in_specs=[vmem] * 3,
        out_specs=(vmem,) * 3,
        scratch_shapes=[pltpu.VMEM((lanes, capacity), f32)],
        compiler_params=pltpu.CompilerParams(vmem_limit_bytes=6 << 20),
        name="tables",
    )(by_slot(energy[0], other_energy[0]), radii[None], matrices)

    packed = pl.pallas_call(
        pack_kernel,
        out_shape=jax.ShapeDtypeStruct((group, rows, capacity + lanes), f32),
        in_specs=[smem, hbm, hbm],
        out_specs=vmem,
        scratch_shapes=[
            pltpu.VMEM((lanes, lanes), f32),
            pltpu.VMEM((capacity, columns), f32),
            pltpu.VMEM((orders, block), f32),
            pltpu.SemaphoreType.DMA((2,)),
        ],
        compiler_params=pltpu.CompilerParams(vmem_limit_bytes=4 << 20),
        name="pack",
    )(
        counts,
        pltpu.with_memory_space_constraint(start_amplitudes.reshape(capacity, columns), pltpu.HBM),
        pltpu.with_memory_space_constraint(radial_terms, pltpu.HBM),
    )
    wide = [[e * group + d for d in range(group)] for e in range(elements)]
    gathered = lax.all_to_all(
        packed.astype(f16), "rad", split_axis=0, concat_axis=0, tiled=True, axis_index_groups=wide
    ).reshape(group * rows, capacity + lanes)
    other_gathered = lax.ppermute(gathered, "sym", swap)

    def by_order(x):
        return pltpu.with_memory_space_constraint(x[0].transpose(0, 2, 1, 3), pltpu.HBM)

    def body(*refs):
        steps_kernel(orders, block, *refs)

    result = pl.pallas_call(
        body,
        out_shape=jax.ShapeDtypeStruct((states, rows, capacity), bf16),
        in_specs=[smem, hbm, hbm] + [vmem] * 6,
        out_specs=vmem,
        scratch_shapes=[
            pltpu.VMEM((2, tiles, orders, tile, 2 * capacity), bf16),
            pltpu.VMEM((2 * capacity, 2 * width), bf16),
            pltpu.VMEM((2 * capacity, 2 * width), bf16),
            pltpu.VMEM((2 * capacity, 2 * width), f32),
            pltpu.VMEM((8, 2 * width), f32),
            pltpu.VMEM((2 * width, capacity), f32),
            pltpu.SemaphoreType.DMA((2, tiles, 2)),
        ],
        compiler_params=pltpu.CompilerParams(vmem_limit_bytes=28 << 20),
        name="steps",
    )(
        info,
        by_order(coupling),
        by_order(other_coupling),
        gathered.astype(f32),
        other_gathered.astype(f32),
        one_half,
        two_half,
        phases,
        masks,
    )
    mine = (place % group) // spread
    received = []
    for turn in range(states - 1, 0, -1):
        pairs = [
            (e * group + n * spread + d, e * group + (n ^ turn) * spread + d)
            for e in range(elements)
            for n in range(states)
            for d in range(spread)
        ]
        piece = lax.dynamic_index_in_dim(result, mine ^ turn, 0, keepdims=False)
        received.insert(0, lax.ppermute(piece, "rad", pairs))
    out = pl.pallas_call(
        unpack_kernel,
        out_shape=jax.ShapeDtypeStruct((capacity, columns), f32),
        in_specs=[smem] + [vmem] * states,
        out_specs=hbm,
        scratch_shapes=[
            pltpu.VMEM((columns, capacity), f32),
            pltpu.VMEM((capacity, columns), f32),
            pltpu.SemaphoreType.DMA((capacity // columns,)),
        ],
        compiler_params=pltpu.CompilerParams(vmem_limit_bytes=4 << 20),
        name="unpack",
    )(mine.astype(jnp.int32)[None], result, *received)
    return out.reshape(start_amplitudes.shape)


def solution(mesh):
    paired = mesh.shape["sym"] == 2

    def program(*args):
        states = args[0].shape[3] // (2 * args[4].shape[1])
        group = args[7].shape[2] // args[4].shape[1]
        if paired and group % states == 0 and states & (states - 1) == 0:
            return pair_shards(*args)
        return halo_shards(*args)

    return jax.shard_map(
        program,
        mesh=mesh,
        in_specs=(
            P("sym", None, "rad", None),
            P("sym", None, None, None, None),
            P("sym", None, None, None),
            P("sym"),
            P(None, "rad"),
            P("sym", None),
            P(),
            P(),
        ),
        out_specs=P("sym", None, "rad", None),
        check_vma=False,
    )
```
